128 devices in a mesh: cfg: 2 (over y_hi), group: 16 (over y_lo, x, core), mp: 4 (over z).
Axes of the slice: x: 4, y: 4 (y_hi: 2, y_lo: 2; y = y_hi * 2 + y_lo), z: 4, core: 2. Of those that a mesh axis runs over, the one named last changes fastest.
Arguments:
- latents: float32 [16384, 64], P(('group', 'mp')), may hold values from -0.6 to 0.6
- text_hidden: bfloat16 [2, 8192, 3072], P('cfg', ('group', 'mp')), may hold values from -6 to 6
- w_img_in: bfloat16 [64, 3072], replicated, may hold values from -0.75 to 0.75
- w_img_qkv: bfloat16 [3072, 4608], P(None, 'mp'), may hold values from -1 to 1
- w_txt_kv: bfloat16 [3072, 3072], P(None, 'mp'), may hold values from -0.109375 to 0.109375
- q_gain: float32 [128], replicated, may hold values from 0.25 to 1.75
- k_gain: float32 [128], replicated, may hold values from 0.25 to 1.75
- w_out: bfloat16 [1536, 3072], replicated, may hold values from -1 to 1
- w_final: bfloat16 [3072, 64], replicated, may hold values from -0.109375 to 0.109375
- mod_img: float32 [8, 3, 3072], replicated, may hold values from -3 to 3
- mod_txt: float32 [8, 2, 3072], replicated, may hold values from -3 to 3
- mod_final: float32 [8, 2, 3072], replicated, may hold values from -3 to 3
- guide: float32 [16], replicated, may hold values from 1.5 to 5
- step_size: float32 [8], replicated, may hold values from 0.02 to 0.3
- img_len: int32 [16], replicated, may hold values from 1 to 1024, as said below
- txt_len: int32 [16], replicated, may hold values from 1 to 512, as said below
- split_flag: int32 [2, 16], replicated, may hold values from 0 to 1, as said below
- tstep: int32 [16], replicated, may hold values from 0 to 7
Outputs:
- velocity: float32 [2, 8192, 64], P('cfg', ('group', 'mp'))
- next_latents: float32 [2, 8192, 64], P('cfg', ('group', 'mp'))
The draws below stay inside these ranges and needn't reach their ends.
Inputs may be any that keep to these rules, and one draw needn't show every extreme that they name: `img_len`: some group has exactly 1024 live image tokens. `txt_len`: some group has exactly 512 live text tokens. `split_flag`: entries [c, 2j] and [c, 2j + 1] are equal; at least one such pair carries 1 and at least one carries 0.
All inputs are finite; a program needn't handle non-finite values.
Results may differ from the reference program's by a relative error of at most 0.035.
Values may be sent and summed in bfloat16 or wider, within the bound.
A program may use at most 192 MiB of HBM per device.

```python
import math
import jax
import jax.numpy as jnp
from jax import lax

D = 3072
HD = 128
CH = 64
HEADS = 12
NT = 8
IMG = 1024
TXT = 512
GROUPS = 16
N_MP = 4


def bounded_lengths(key, most):
    first, second = jax.random.split(key)
    values = jax.random.randint(first, (GROUPS,), 1, most + 1)
    chosen = jax.random.randint(second, (), 0, GROUPS)
    return jnp.where(jnp.arange(GROUPS) == chosen, most, values).astype(jnp.int32)


def draw_img_len(key, part):
    return bounded_lengths(jax.random.fold_in(key, 11), IMG)


def draw_txt_len(key, part):
    return bounded_lengths(jax.random.fold_in(key, 12), TXT)


def draw_split_flag(key, part):
    first, second, third = jax.random.split(jax.random.fold_in(key, 13), 3)
    pair_count = GROUPS
    paired = jax.random.randint(first, (pair_count,), 0, 2)
    chosen_on = jax.random.randint(second, (), 0, pair_count)
    offset = jax.random.randint(third, (), 1, pair_count)
    chosen_off = (chosen_on + offset) % pair_count
    pair_ids = jnp.arange(pair_count)
    paired = jnp.where(pair_ids == chosen_on, 1, paired)
    paired = jnp.where(pair_ids == chosen_off, 0, paired)
    return jnp.repeat(paired.reshape(2, GROUPS // 2), 2, axis=1).astype(jnp.int32)


def draw_mod_img(key, part):
    first, second, third = jax.random.split(jax.random.fold_in(key, 31), 3)
    shifts = 0.5 * jax.random.truncated_normal(first, -6.0, 6.0, (NT, 2, D), jnp.float32)
    sizes = jax.random.uniform(second, (NT, 1, D), jnp.float32, 1.5, 3.0)
    signs = jnp.where(jax.random.bernoulli(third, 0.5, (NT, 1, D)), 1.0, -1.0).astype(jnp.float32)
    return jnp.concatenate([shifts, signs * sizes], axis=1).astype(jnp.float32)


def draw_w_img_qkv(key, part):
    first = jax.random.fold_in(jax.random.fold_in(key, 32), 0)
    own = jax.random.truncated_normal(first, -4.0, 4.0, (D, HEADS, 3 * HD), jnp.float32)
    return (own * D ** (-0.5)).reshape(D, 3 * HEADS * HD).astype(jnp.bfloat16)


def draw_w_out(key, part):
    first = jax.random.fold_in(jax.random.fold_in(key, 33), 0)
    own = jax.random.truncated_normal(first, -4.0, 4.0, (HEADS, HD, D), jnp.float32)
    return (own * (HEADS * HD) ** (-0.5)).reshape(HEADS * HD, D).astype(jnp.bfloat16)


def with_ends(entries, stream_key, smallest, largest):
    index_at = [jax.random.randint(jax.random.fold_in(stream_key, axis), (), 0, length) for axis, length in enumerate(entries.shape)]
    widest = entries.shape.index(max(entries.shape))
    beside = index_at[:widest] + [(index_at[widest] + 1) % entries.shape[widest]] + index_at[widest + 1:]
    return entries.at[tuple(index_at)].set(smallest).at[tuple(beside)].set(largest)


def steps_of(rng, shape, cuts, least, largest):
    factor_of = 1.0
    for dim, shards_of in cuts:
        draws = jax.random.uniform(jax.random.fold_in(jax.random.fold_in(rng, 6), dim), (shards_of,), jnp.float32, least / len(cuts), largest / len(cuts))
        factor_of = factor_of * jnp.repeat(jnp.exp(draws), shape[dim] // shards_of).reshape((-1,) + (1,) * (len(shape) - 1 - dim))
    return factor_of


def normal_values(own_key, shape, deviation, most, pieces=(), held_as=jnp.bfloat16):
    result = deviation * jax.random.normal(own_key, shape, jnp.float32)
    if pieces:
        result = result * steps_of(own_key, shape, pieces, -0.22, 0.18)
    return jnp.clip(result, -most, most).astype(held_as)


def setup_inputs(seed: int = 0) -> dict:
    keys = jax.random.split(jax.random.key(seed), 19)
    latents = normal_values(keys[0], (GROUPS * IMG, CH), 0.1, 0.6, ((0, 64),), jnp.float32)
    text_hidden = normal_values(keys[1], (2, GROUPS * TXT, D), 1.0, 6.0, ((0, 2), (1, 64)))
    w_img_in = normal_values(keys[2], (CH, D), CH ** -0.5, 0.75)
    w_img_qkv = draw_w_img_qkv(jax.random.fold_in(keys[18], 71), 0)
    w_txt_kv = normal_values(keys[4], (D, 2 * HEADS * HD), D ** -0.5, 0.109375, ((1, 4),))
    q_gain = jnp.clip(1.0 + 0.15 * jax.random.normal(keys[5], (HD,), jnp.float32), 0.25, 1.75)
    k_gain = jnp.clip(1.0 + 0.15 * jax.random.normal(keys[6], (HD,), jnp.float32), 0.25, 1.75)
    w_out = draw_w_out(jax.random.fold_in(keys[18], 71), 0)
    w_final = normal_values(keys[8], (D, CH), D ** -0.5, 0.109375)
    mod_img = draw_mod_img(jax.random.fold_in(keys[18], 71), 0)
    mod_txt = normal_values(keys[10], (NT, 2, D), 0.5, 3.0, (), jnp.float32)
    mod_final = normal_values(keys[11], (NT, 2, D), 0.5, 3.0, (), jnp.float32)
    guide = jnp.clip(jax.random.uniform(keys[12], (GROUPS,), jnp.float32, 1.5, 5.0), 1.5, 5.0)
    step_size = jnp.clip(jnp.exp(jax.random.uniform(keys[13], (NT,), jnp.float32, math.log(0.02), math.log(0.3))), 0.02, 0.3)
    img_len = draw_img_len(jax.random.fold_in(keys[18], 71), 0)
    txt_len = draw_txt_len(jax.random.fold_in(keys[18], 71), 0)
    split_flag = draw_split_flag(jax.random.fold_in(keys[18], 71), 0)
    tstep = with_ends(jax.random.randint(keys[17], (GROUPS,), 0, NT), jax.random.fold_in(keys[17], 1), 0, NT - 1).astype(jnp.int32)
    return {"latents": latents, "text_hidden": text_hidden, "w_img_in": w_img_in, "w_img_qkv": w_img_qkv, "w_txt_kv": w_txt_kv, "q_gain": q_gain, "k_gain": k_gain, "w_out": w_out, "w_final": w_final, "mod_img": mod_img, "mod_txt": mod_txt, "mod_final": mod_final, "guide": guide, "step_size": step_size, "img_len": img_len, "txt_len": txt_len, "split_flag": split_flag, "tstep": tstep}


def layer_norm(values):
    center = values - lax.optimization_barrier(jnp.mean(values, -1, keepdims=True))
    spread = lax.optimization_barrier(jnp.mean(center * center, -1, keepdims=True))
    return center * lax.rsqrt(spread + 1e-06)

def head_norm(values, gain):
    return values * lax.rsqrt(lax.optimization_barrier(jnp.mean(values * values, -1, keepdims=True)) + 1e-06) * gain

def arrange_rows(values):
    half_rows = IMG // (2 * N_MP)
    split_rows = values.reshape(GROUPS, N_MP, 2, half_rows, CH)
    return jnp.transpose(split_rows, (2, 0, 1, 3, 4)).reshape(2, GROUPS * IMG // 2, CH)

def reference(latents, text_hidden, w_img_in, w_img_qkv, w_txt_kv, q_gain, k_gain, w_out, w_final, mod_img, mod_txt, mod_final, guide, step_size, img_len, txt_len, split_flag, tstep):
    x_img = jnp.dot(latents.astype(jnp.bfloat16), w_img_in, preferred_element_type=jnp.float32).reshape(GROUPS, IMG, D)
    mod_rows = mod_img[tstep]
    img_mod = (layer_norm(x_img) * (1.0 + mod_rows[:, 1:2]) + mod_rows[:, 0:1]).astype(jnp.bfloat16)
    text_rows = mod_txt[tstep]
    texts = text_hidden.astype(jnp.float32).reshape(2, GROUPS, TXT, D)
    txt_mod = (layer_norm(texts) * (1.0 + text_rows[None, :, 1:2]) + text_rows[None, :, 0:1]).astype(jnp.bfloat16)
    qkv = jnp.dot(img_mod.reshape(GROUPS * IMG, D), w_img_qkv, preferred_element_type=jnp.float32).reshape(GROUPS, IMG, HEADS, 3, HD)
    query = head_norm(qkv[..., 0, :], q_gain).astype(jnp.bfloat16)
    key_img = head_norm(qkv[..., 1, :], k_gain).astype(jnp.bfloat16)
    value_img = qkv[..., 2, :].astype(jnp.bfloat16)
    text_kv = jnp.dot(txt_mod.reshape(2 * GROUPS * TXT, D), w_txt_kv, preferred_element_type=jnp.float32).reshape(2, GROUPS, TXT, HEADS, 2, HD)
    key_txt = head_norm(text_kv[..., 0, :], k_gain).astype(jnp.bfloat16)
    value_txt = text_kv[..., 1, :].astype(jnp.bfloat16)
    key_all = jnp.concatenate([key_txt, jnp.broadcast_to(key_img[None], (2,) + key_img.shape)], axis=2)
    value_all = jnp.concatenate([value_txt, jnp.broadcast_to(value_img[None], (2,) + value_img.shape)], axis=2)
    spots_txt = jnp.arange(TXT, dtype=jnp.int32)
    spots_img = jnp.arange(IMG, dtype=jnp.int32)
    valid = jnp.concatenate([spots_txt[None, :] < txt_len[:, None], spots_img[None, :] < img_len[:, None]], axis=1)
    final_rows = mod_final[tstep]

    def one_item(index):
        side = index // GROUPS
        group = index % GROUPS
        mate = jnp.bitwise_xor(group, 1)
        key_rows = jnp.concatenate([key_all[side, group], key_all[side, mate]], axis=0)
        value_rows = jnp.concatenate([value_all[side, group], value_all[side, mate]], axis=0)
        live = jnp.concatenate([valid[group], valid[mate] & (split_flag[side, group] == 1)])
        scores = jnp.einsum('qhe,khe->hqk', query[group].astype(jnp.float32), key_rows.astype(jnp.float32)) * HD ** (-0.5)
        scores = jnp.where(live[None, None, :], scores, -1e+30)
        weights = jnp.exp(scores - lax.optimization_barrier(jnp.max(scores, -1, keepdims=True)))
        probs = (weights / lax.optimization_barrier(jnp.sum(weights, -1, keepdims=True))).astype(jnp.bfloat16)
        mixed = jnp.einsum('hqk,khe->qhe', probs.astype(jnp.float32), value_rows.astype(jnp.float32)).astype(jnp.bfloat16)
        attended = jnp.dot(mixed.reshape(IMG, HEADS * HD), w_out, preferred_element_type=jnp.float32)
        hidden = x_img[group] + mod_rows[group, 2] * attended
        final = (layer_norm(hidden) * (1.0 + final_rows[group, 1]) + final_rows[group, 0]).astype(jnp.bfloat16)
        return jnp.dot(final, w_final, preferred_element_type=jnp.float32)
    vel = lax.map(one_item, jnp.arange(2 * GROUPS, dtype=jnp.int32)).reshape(2, GROUPS, IMG, CH)
    guided = vel[1] + guide[:, None, None] * (vel[0] - vel[1])
    row_live = spots_img[None, :] < img_len[:, None]
    guided = jnp.where(row_live[:, :, None], guided, 0.0)
    start = latents.reshape(GROUPS, IMG, CH)
    moved = start - step_size[tstep][:, None, None] * guided
    return (arrange_rows(guided), arrange_rows(moved))
```

```python
import jax
import jax.numpy as jnp
from jax import lax
from jax.sharding import PartitionSpec as P

HD = 128


def partner(value, axis, bit):
    mask = 2**bit
    pairs = [(source, source ^ mask) for source in range(lax.axis_size(axis))]
    return lax.ppermute(value, axis, pairs)


def layer_norm(values):
    center = values - jnp.mean(values, -1, keepdims=True)
    spread = jnp.mean(center * center, -1, keepdims=True)
    return center * lax.rsqrt(spread + 1e-06)


def head_norm(values, gain):
    return values * lax.rsqrt(jnp.mean(values * values, -1, keepdims=True) + 1e-06) * gain


def pick_entry(table, index):
    return lax.dynamic_index_in_dim(table, index, 0, keepdims=False)


def local(
    latents,
    text_hidden,
    w_img_in,
    w_img_qkv,
    w_txt_kv,
    q_gain,
    k_gain,
    w_out,
    w_final,
    mod_img,
    mod_txt,
    mod_final,
    guide,
    step_size,
    img_len,
    txt_len,
    split_flag,
    tstep,
):
    group_index = lax.axis_index("group")
    mp_index = lax.axis_index("mp")
    cfg_index = lax.axis_index("cfg")
    mp_count = lax.axis_size("mp")
    mate_index = jnp.bitwise_xor(group_index, 1)
    step_index = pick_entry(tstep, group_index)
    mod_rows = pick_entry(mod_img, step_index)
    text_rows = pick_entry(mod_txt, step_index)
    final_rows = pick_entry(mod_final, step_index)
    shard_rows = latents.shape[0]
    half_rows = shard_rows // 2
    full_img = shard_rows * mp_count
    full_txt = text_hidden.shape[1] * mp_count
    local_heads = w_img_qkv.shape[1] // (3 * HD)
    x_img = jnp.dot(latents.astype(jnp.bfloat16), w_img_in, preferred_element_type=jnp.float32)
    lat_full = lax.all_gather(latents.astype(jnp.bfloat16), "mp", axis=0, tiled=True)
    x_full = jnp.dot(lat_full, w_img_in, preferred_element_type=jnp.float32)
    img_full = (layer_norm(x_full) * (1.0 + mod_rows[1]) + mod_rows[0]).astype(jnp.bfloat16)
    txt_mod = (
        layer_norm(text_hidden[0].astype(jnp.float32)) * (1.0 + text_rows[1]) + text_rows[0]
    ).astype(jnp.bfloat16)
    txt_full = lax.all_gather(txt_mod, "mp", axis=0, tiled=True)
    qkv = jnp.dot(img_full, w_img_qkv, preferred_element_type=jnp.float32).reshape(
        full_img, local_heads, 3, HD
    )
    query = head_norm(qkv[:, :, 0], q_gain).astype(jnp.bfloat16)
    key_img = head_norm(qkv[:, :, 1], k_gain).astype(jnp.bfloat16)
    value_img = qkv[:, :, 2].astype(jnp.bfloat16)
    text_kv = jnp.dot(txt_full, w_txt_kv, preferred_element_type=jnp.float32).reshape(
        full_txt, local_heads, 2, HD
    )
    key_txt = head_norm(text_kv[:, :, 0], k_gain).astype(jnp.bfloat16)
    value_txt = text_kv[:, :, 1].astype(jnp.bfloat16)
    key_rows = jnp.concatenate([key_txt, key_img], axis=0)
    value_rows = jnp.concatenate([value_txt, value_img], axis=0)
    mate_keys, mate_values = partner((key_rows, value_rows), "group", 0)
    spots_txt = jnp.arange(full_txt, dtype=jnp.int32)
    spots_img = jnp.arange(full_img, dtype=jnp.int32)

    def live_rows(index):
        return jnp.concatenate(
            [spots_txt < pick_entry(txt_len, index), spots_img < pick_entry(img_len, index)]
        )

    flagged = pick_entry(pick_entry(split_flag, cfg_index), group_index) == 1
    live = jnp.concatenate([live_rows(group_index), live_rows(mate_index) & flagged])
    all_keys = jnp.concatenate([key_rows, mate_keys], axis=0)
    all_values = jnp.concatenate([value_rows, mate_values], axis=0)
    scores = jnp.einsum(
        "qhe,khe->hqk", query, all_keys, preferred_element_type=jnp.float32
    ) * HD ** (-0.5)
    scores = jnp.where(live[None, None, :], scores, -1e30)
    weights = jnp.exp(scores - jnp.max(scores, -1, keepdims=True))
    probs = (weights / jnp.sum(weights, -1, keepdims=True)).astype(jnp.bfloat16)
    mixed = jnp.einsum(
        "hqk,khe->qhe", probs, all_values, preferred_element_type=jnp.float32
    ).astype(jnp.bfloat16)
    mixed = mixed.reshape(full_img, local_heads * HD)
    mixed = lax.all_to_all(mixed, "mp", split_axis=0, concat_axis=1, tiled=True)
    attended = jnp.dot(mixed, w_out, preferred_element_type=jnp.float32)
    hidden = x_img + mod_rows[2] * attended
    final = (layer_norm(hidden) * (1.0 + final_rows[1]) + final_rows[0]).astype(jnp.bfloat16)
    own_velocity = jnp.dot(final, w_final, preferred_element_type=jnp.float32)
    scale = pick_entry(guide, group_index)
    other_velocity = partner(own_velocity.astype(jnp.bfloat16), "cfg", 0).astype(own_velocity.dtype)
    is_cond = cfg_index == 0
    cond_part = jnp.where(is_cond, own_velocity, other_velocity)
    uncond_part = jnp.where(is_cond, other_velocity, own_velocity)
    guided_all = uncond_part + scale * (cond_part - uncond_part)
    guided = lax.dynamic_slice_in_dim(guided_all, cfg_index * half_rows, half_rows, 0)
    row_place = (
        mp_index * shard_rows + cfg_index * half_rows + jnp.arange(half_rows, dtype=jnp.int32)
    )
    row_live = row_place < pick_entry(img_len, group_index)
    guided = jnp.where(row_live[:, None], guided, 0.0)
    start_rows = lax.dynamic_slice_in_dim(latents, cfg_index * half_rows, half_rows, 0)
    moved = start_rows - pick_entry(step_size, step_index) * guided
    return (guided[None], moved[None])


def solution(mesh):
    placed = (
        P(("group", "mp"), None),
        P("cfg", ("group", "mp"), None),
        P(),
        P(None, "mp"),
        P(None, "mp"),
        P(),
        P(),
        P(),
        P(),
        P(),
        P(),
        P(),
        P(),
        P(),
        P(),
        P(),
        P(),
        P(),
    )
    return jax.shard_map(
        local,
        mesh=mesh,
        in_specs=placed,
        out_specs=(P("cfg", ("group", "mp"), None), P("cfg", ("group", "mp"), None)),
        check_vma=False,
    )
```

```python
import functools
import math

import jax
import jax.numpy as jnp
from jax import lax
from jax.experimental import pallas as pl
from jax.experimental.pallas import tpu as pltpu
from jax.sharding import PartitionSpec as P

HD = 128
F32 = jnp.float32
BF16 = jnp.bfloat16
MESH = pl.DeviceIdType.MESH
TEXT_FROM = (0, 1, 3, 2)


def nt_dot(a, b):
    return lax.dot_general(a, b, (((1,), (1,)), ((), ())), preferred_element_type=F32)


def dot(a, b):
    return jnp.dot(a, b, preferred_element_type=F32)


def head_norm(values, gain):
    return values * lax.rsqrt(jnp.mean(values * values, -1, keepdims=True) + 1e-06) * gain


def split(values):
    high = values.astype(BF16)
    return high, (values - high.astype(F32)).astype(BF16)


def body(
    lat_h, text_h, win_h, wq_h, wt_h, wo_h, wf_h, mimg_h, mtxt_h, mfin_h,
    qg, kg, guide, step_size, img_len, txt_len, flags, tstep,
    vel_o, next_o,
    lat, text, win, wq, wt, wo, wf, mimg, mtxt, mfin,
    txt, lall, wx, lhs, rhs, bias, xc, q, kv, kvm, mask, maskm, acc, att,
    mix, mixr, relay, fin, vsend, vrecv,
    lsem, ts, tr, ls, lr, ks, kr, ms, mr, vs, vr,
):
    c = lax.axis_index("cfg")
    g = lax.axis_index("group")
    m = lax.axis_index("mp")
    n_mp = 4
    right, left = lax.rem(m + 1, n_mp), lax.rem(m + 3, n_mp)
    mate = g + 1 - 2 * lax.rem(g, 2)
    rows, ch = lat_h.shape
    trows, d = text_h.shape
    heads = wq_h.shape[1] // (3 * HD)
    img, ntxt = rows * n_mp, trows * n_mp
    half = rows // 2
    part = trows // 4

    def local_copy(src, dst, i):
        copy = pltpu.make_async_copy(src, dst, lsem.at[i])
        copy.start()
        return copy

    c_text = local_copy(text_h, text, 0)
    c_mtxt = local_copy(mtxt_h, mtxt, 1)
    c_lat = local_copy(lat_h, lat, 2)
    c_win = local_copy(win_h, win, 3)
    c_mimg = local_copy(mimg_h, mimg, 4)
    c_wq = [
        local_copy(wq_h.at[:, pl.ds(h * 3 * HD, 3 * HD)], wq.at[h], 5 + h) for h in range(heads)
    ]
    c_wt = local_copy(wt_h, wt, 5 + heads)
    c_wo = local_copy(wo_h, wo, 6 + heads)
    c_wf = local_copy(wf_h, wf, 7 + heads)
    c_mfin = local_copy(mfin_h, mfin, 8 + heads)

    barrier = pltpu.get_barrier_semaphore()
    for k in (1, 2, 3):
        pl.semaphore_signal(
            barrier, inc=1, device_id={"mp": lax.rem(m + k, n_mp)}, device_id_type=MESH
        )
    pl.semaphore_signal(barrier, inc=1, device_id={"group": mate}, device_id_type=MESH)
    pl.semaphore_signal(barrier, inc=1, device_id={"cfg": 1 - c}, device_id_type=MESH)

    def remote(src, dst, ssem, rsem, device):
        return pltpu.make_async_remote_copy(
            src_ref=src, dst_ref=dst, send_sem=ssem, recv_sem=rsem,
            device_id=device, device_id_type=MESH,
        )

    step = tstep[g]
    il, tl = img_len[g], txt_len[g]
    il_m, tl_m = img_len[mate], txt_len[mate]
    flag = jnp.where(flags[c, g] == 1, 1.0, 0.0).astype(F32)

    def chunk(i):
        return pl.ds(i * part, part)

    to_right = [
        remote(txt.at[0, chunk(i)], txt.at[2, chunk(i)], ts.at[i], tr.at[i], {"mp": right})
        for i in range(4)
    ]
    to_left = [
        remote(txt.at[0, chunk(i)], txt.at[1, chunk(i)], ts.at[4 + i], tr.at[4 + i], {"mp": left})
        for i in range(4)
    ]
    on_right = [
        remote(txt.at[2, chunk(i)], txt.at[3, chunk(i)], ts.at[8 + i], tr.at[8 + i], {"mp": right})
        for i in (0, 1)
    ]
    on_left = [
        remote(txt.at[1, chunk(i)], txt.at[3, chunk(i)], ts.at[8 + i], tr.at[8 + i], {"mp": left})
        for i in (2, 3)
    ]

    def norm_text(i):
        x = text[chunk(i), :].astype(F32)
        center = x - jnp.mean(x, -1, keepdims=True)
        spread = jnp.mean(center * center, -1, keepdims=True)
        y = center * lax.rsqrt(spread + 1e-06) * (1.0 + mtxt[step, 1:2, :]) + mtxt[step, 0:1, :]
        txt[0, chunk(i), :] = y.astype(BF16)

    c_text.wait()
    c_mtxt.wait()
    norm_text(0)
    norm_text(2)
    pl.semaphore_wait(barrier, 5)
    to_right[0].start()
    to_left[2].start()

    c_lat.wait()
    c_win.wait()
    c_mimg.wait()
    e_row = lax.broadcasted_iota(jnp.int32, (ch, 2 * ch), 0)
    e_col = lax.broadcasted_iota(jnp.int32, (ch, 2 * ch), 1)
    twice = jnp.where((e_col == e_row) | (e_col == e_row + ch), 1.0, 0.0).astype(BF16)
    lat2 = dot(lat[...].astype(BF16), twice)
    w = win[...].astype(F32)
    w = w - jnp.mean(w, -1, keepdims=True)
    w_high, w_low = split(w)
    wx[0:ch, :] = w_high
    wx[ch : 2 * ch, :] = w_low
    s_high, s_low = split(w * (1.0 + mimg[step, 1:2, :]))
    lhs[0:ch, :] = s_high
    lhs[ch : 2 * ch, :] = s_low
    b_high, b_low = split(mimg[step, 0:1, :])
    b_row = lax.broadcasted_iota(jnp.int32, (16, d), 0)
    lhs[2 * ch :, :] = jnp.where(
        b_row == 0, b_high.astype(F32), jnp.where(b_row == 1, b_low.astype(F32), 0.0)
    ).astype(BF16)
    lat2b = lat2.astype(BF16)
    squares = jnp.zeros((rows, HD), F32)
    wide = min(d, 512)
    for j in range(d // wide):
        x = dot(lat2b, wx[:, j * wide : (j + 1) * wide])
        xc[:, j * wide : (j + 1) * wide] = x
        for k in range(wide // HD):
            piece = x[:, k * HD : (k + 1) * HD]
            squares = squares + piece * piece
    rstd = lax.rsqrt(jnp.sum(squares, -1, keepdims=True) / d + 1e-06)
    scaled = lat2 * rstd
    scaled_high = scaled.astype(BF16).astype(F32)
    lane = lax.broadcasted_iota(jnp.int32, (rows, 2 * ch), 1)
    lall[0] = jnp.where(lane < ch, scaled_high, scaled - scaled_high).astype(BF16)
    lat_out = [
        remote(
            lall.at[0], lall.at[4 - k], ls.at[k - 1], lr.at[k - 1], {"mp": lax.rem(m + k, n_mp)}
        )
        for k in (1, 2, 3)
    ]
    for copy in lat_out:
        copy.start()

    norm_text(1)
    norm_text(3)
    to_right[1].start()
    to_left[3].start()
    to_right[2].start()
    to_left[0].start()
    to_right[3].start()
    to_left[1].start()

    def fill_mask(ref, img_live, txt_live):
        spot = lax.broadcasted_iota(jnp.int32, (rows, HD), 0)
        for k in range(4):
            start = lax.rem(m + k, n_mp) * rows
            ref[k * rows : (k + 1) * rows, :] = jnp.where(
                spot + start < img_live, 1.0, 0.0
            ).astype(BF16)
        spot_t = lax.broadcasted_iota(jnp.int32, (trows, HD), 0)
        for k in range(4):
            start = lax.rem(m + TEXT_FROM[k], n_mp) * trows
            ref[img + k * trows : img + (k + 1) * trows, :] = jnp.where(
                spot_t + start < txt_live, 1.0, 0.0
            ).astype(BF16)

    fill_mask(mask, il, tl)
    fill_mask(maskm, il_m, tl_m)

    for h in range(heads):
        c_wq[h].wait()
        full = dot(lhs[...], wq[h])
        fold = full[0:ch] + full[ch : 2 * ch]
        high, low = split(fold)
        rhs[h, 0:ch, :] = high
        rhs[h, ch : 2 * ch, :] = high
        rhs[h, 2 * ch : 3 * ch, :] = low
        rhs[h, 3 * ch : 4 * ch, :] = low
        bias[h] = full[2 * ch : 2 * ch + 8]
    for copy in lat_out:
        copy.wait_recv()
    q_gain = qg[...] * (HD ** (-0.5) * math.log2(math.e))
    k_gain = kg[...]
    kv_img = []
    for h in range(heads):

        def image_block(k, carry, h=h):
            block = lall[k]
            at = pl.ds(pl.multiple_of(k * rows, rows), rows)
            both = bias[h, 0:1, :] + bias[h, 1:2, :]
            x = dot(jnp.concatenate([block, block], axis=1), rhs[h]) + both
            q[h, at, :] = head_norm(x[:, 0:HD], q_gain).astype(BF16)
            kv[h, at, 0:HD] = head_norm(x[:, HD : 2 * HD], k_gain).astype(BF16)
            kv[h, at, HD : 2 * HD] = x[:, 2 * HD :].astype(BF16) * mask[at, :]
            return carry

        lax.fori_loop(0, n_mp, image_block, 0)
        copy = remote(
            kv.at[h, pl.ds(0, img)], kvm.at[h, pl.ds(0, img)], ks.at[h], kr.at[h],
            {"group": mate},
        )
        copy.start()
        kv_img.append(copy)

    def text_block(first, count):
        span = slice(img + first * trows, img + (first + count) * trows)
        lhs_t = txt[first] if count == 1 else jnp.concatenate(
            [txt[first + k] for k in range(count)], axis=0
        )
        for h in range(heads):
            x = dot(lhs_t, wt[:, h * 2 * HD : (h + 1) * 2 * HD])
            kv[h, span, 0:HD] = head_norm(x[:, 0:HD], k_gain).astype(BF16)
            kv[h, span, HD : 2 * HD] = x[:, HD:].astype(BF16) * mask[span, :]
        i = heads + first if first < 2 else heads + 2
        copy = remote(
            kv.at[:, pl.ds(img + first * trows, count * trows)],
            kvm.at[:, pl.ds(img + first * trows, count * trows)],
            ks.at[i], kr.at[i], {"group": mate},
        )
        copy.start()
        return copy

    c_wt.wait()
    kv_txt = [text_block(0, 1)]

    def attend(ref, mref, h, at, lo, n):
        s = nt_dot(q[h, at, :], ref[h, lo : lo + n, 0:HD])
        p = jnp.exp2(s).astype(BF16)
        return dot(
            p, jnp.concatenate([ref[h, lo : lo + n, HD : 2 * HD], mref[lo : lo + n, :]], axis=1)
        )

    def each_block(fn):
        def run(i, carry):
            h, k = i // n_mp, lax.rem(i, n_mp)
            fn(h, pl.ds(pl.multiple_of(k * rows, rows), rows))
            return carry

        lax.fori_loop(0, heads * n_mp, run, 0)

    def own_image(h, at):
        acc[h, at, :] = attend(kv, mask, h, at, 0, img)

    each_block(own_image)

    to_right[0].wait_recv()
    on_right[0].start()
    to_left[2].wait_recv()
    on_left[0].start()
    for copy in kv_img:
        copy.wait_recv()

    def mate_image(h, at):
        acc[h, at, :] += flag * attend(kvm, maskm, h, at, 0, img)

    each_block(mate_image)

    to_right[1].wait_recv()
    on_right[1].start()
    to_left[3].wait_recv()
    on_left[1].start()
    to_right[2].wait_recv()
    to_right[3].wait_recv()
    to_left[0].wait_recv()
    to_left[1].wait_recv()
    kv_txt.append(text_block(1, 2))
    kv_txt[0].wait_recv()
    kv_txt[1].wait_recv()

    def most_text(h, at):
        own = attend(kv, mask, h, at, img, 3 * trows)
        other = attend(kvm, maskm, h, at, img, 3 * trows)
        acc[h, at, :] += own + flag * other

    each_block(most_text)

    for copy in on_right + on_left:
        copy.wait_recv()
    kv_txt.append(text_block(3, 1))
    last = img + 3 * trows

    kv_txt[2].wait_recv()

    def last_block(k):
        at = slice(k * rows, (k + 1) * rows)

        def run(h, carry):
            own = attend(kv, mask, h, at, last, trows)
            other = attend(kvm, maskm, h, at, last, trows)
            total = acc[h, at, :] + own + flag * other
            mix[k, h] = (total[:, 0:HD] / total[:, HD : 2 * HD]).astype(BF16)
            return carry

        lax.fori_loop(0, heads, run, 0)

    first_half, second_half = pl.ds(0, half), pl.ds(half, half)
    hop_a = remote(mix.at[2, :, first_half], relay.at[0], ms.at[0], mr.at[0], {"mp": right})
    hop_b = remote(mix.at[2, :, second_half], relay.at[1], ms.at[1], mr.at[1], {"mp": left})
    mix_r = remote(mix.at[1], mixr.at[2], ms.at[2], mr.at[2], {"mp": right})
    mix_l = remote(mix.at[3], mixr.at[0], ms.at[3], mr.at[3], {"mp": left})
    fwd_a = remote(relay.at[0], mixr.at[1, :, first_half], ms.at[4], mr.at[4], {"mp": right})
    fwd_b = remote(relay.at[1], mixr.at[1, :, second_half], ms.at[5], mr.at[5], {"mp": left})

    last_block(2)
    hop_a.start()
    hop_b.start()
    last_block(1)
    mix_r.start()
    last_block(3)
    mix_l.start()
    last_block(0)
    hop_a.wait_recv()
    fwd_a.start()
    hop_b.wait_recv()
    fwd_b.start()
    c_wo.wait()

    def project(ref, k, first):
        base = pl.multiple_of(lax.rem(m + k, n_mp) * (heads * HD), heads * HD)
        own = jnp.concatenate([ref[h] for h in range(heads)], axis=1)
        for j in range(d // wide):
            cols = slice(j * wide, (j + 1) * wide)
            x = dot(own, wo[pl.ds(base, heads * HD), cols])
            att[:, cols] = x if first else att[:, cols] + x

    project(mix.at[0], 0, True)
    mix_r.wait_recv()
    project(mixr.at[2], 3, False)
    mix_l.wait_recv()
    project(mixr.at[0], 1, False)
    fwd_a.wait_recv()
    fwd_b.wait_recv()
    project(mixr.at[1], 2, False)
    c_wf.wait()
    c_mfin.wait()

    def finish(start):
        small = min(half, 32)

        def run(i, carry):
            at = pl.ds(pl.multiple_of(start + i * small, small), small)
            x = xc[at, :] + mimg[step, 2:3, :] * att[at, :]
            center = x - jnp.mean(x, -1, keepdims=True)
            spread = jnp.mean(center * center, -1, keepdims=True)
            y = center * lax.rsqrt(spread + 1e-06) * (1.0 + mfin[step, 1:2, :]) + mfin[step, 0:1, :]
            fin[pl.ds(pl.multiple_of(i * small, small), small), :] = y.astype(BF16)
            return carry

        lax.fori_loop(0, half // small, run, 0)
        return dot(fin[...], wf[...])

    vsend[...] = finish(pl.multiple_of((1 - c) * half, half))
    swap = remote(vsend, vrecv, vs.at[0], vr.at[0], {"cfg": 1 - c})
    swap.start()
    own = finish(pl.multiple_of(c * half, half))
    swap.wait_recv()
    other = vrecv[...]
    cond = jnp.where(c == 0, own, other)
    uncond = jnp.where(c == 0, other, own)
    guided = uncond + guide[g] * (cond - uncond)
    spot = lax.broadcasted_iota(jnp.int32, (half, ch), 0) + (m * rows + c * half)
    guided = jnp.where(spot < il, guided, 0.0)
    vel_o[...] = guided
    next_o[...] = lat[pl.ds(pl.multiple_of(c * half, half), half), :] - step_size[step] * guided

    for copy in to_right + to_left + on_right + on_left + lat_out + kv_img + kv_txt:
        copy.wait_send()
    for copy in (hop_a, hop_b, mix_r, mix_l, fwd_a, fwd_b, swap):
        copy.wait_send()


def local(
    latents, text_hidden, w_img_in, w_img_qkv, w_txt_kv, q_gain, k_gain, w_out, w_final,
    mod_img, mod_txt, mod_final, guide, step_size, img_len, txt_len, split_flag, tstep,
):
    text = text_hidden[0]
    rows, ch = latents.shape
    trows, d = text.shape
    heads = w_img_qkv.shape[1] // (3 * HD)
    img, ntxt = 4 * rows, 4 * trows
    half = rows // 2
    hbm = pl.BlockSpec(memory_space=pl.ANY)
    vmem = pl.BlockSpec(memory_space=pltpu.VMEM)
    smem = pl.BlockSpec(memory_space=pltpu.SMEM)
    dma = pltpu.SemaphoreType.DMA
    out = jax.ShapeDtypeStruct((half, ch), F32)
    scratch = [
        pltpu.VMEM(latents.shape, F32),
        pltpu.VMEM(text.shape, BF16),
        pltpu.VMEM(w_img_in.shape, BF16),
        pltpu.VMEM((heads, d, 3 * HD), BF16),
        pltpu.VMEM(w_txt_kv.shape, BF16),
        pltpu.VMEM(w_out.shape, BF16),
        pltpu.VMEM(w_final.shape, BF16),
        pltpu.VMEM(mod_img.shape, F32),
        pltpu.VMEM(mod_txt.shape, F32),
        pltpu.VMEM(mod_final.shape, F32),
        pltpu.VMEM((4, trows, d), BF16),
        pltpu.VMEM((4, rows, 2 * ch), BF16),
        pltpu.VMEM((2 * ch, d), BF16),
        pltpu.VMEM((2 * ch + 16, d), BF16),
        pltpu.VMEM((heads, 4 * ch, 3 * HD), BF16),
        pltpu.VMEM((heads, 8, 3 * HD), F32),
        pltpu.VMEM((rows, d), F32),
        pltpu.VMEM((heads, img, HD), BF16),
        pltpu.VMEM((heads, img + ntxt, 2 * HD), BF16),
        pltpu.VMEM((heads, img + ntxt, 2 * HD), BF16),
        pltpu.VMEM((img + ntxt, HD), BF16),
        pltpu.VMEM((img + ntxt, HD), BF16),
        pltpu.VMEM((heads, img, 2 * HD), F32),
        pltpu.VMEM((rows, d), F32),
        pltpu.VMEM((4, heads, rows, HD), BF16),
        pltpu.VMEM((3, heads, rows, HD), BF16),
        pltpu.VMEM((2, heads, half, HD), BF16),
        pltpu.VMEM((half, d), BF16),
        pltpu.VMEM((half, ch), F32),
        pltpu.VMEM((half, ch), F32),
        dma((9 + heads,)),
        dma((12,)), dma((12,)),
        dma((3,)), dma((3,)),
        dma((heads + 3,)), dma((heads + 3,)),
        dma((6,)), dma((6,)),
        dma((1,)), dma((1,)),
    ]
    velocity, moved = pl.pallas_call(
        body,
        out_shape=(out, out),
        in_specs=[hbm] * 10 + [vmem] * 2 + [smem] * 6,
        out_specs=(vmem, vmem),
        scratch_shapes=scratch,
        compiler_params=pltpu.CompilerParams(
            collective_id=0, has_side_effects=True, vmem_limit_bytes=61 * 1024 * 1024
        ),
        name="guided_step",
    )(
        latents, text, w_img_in, w_img_qkv, w_txt_kv, w_out, w_final, mod_img, mod_txt, mod_final,
        q_gain[None], k_gain[None], guide, step_size, img_len, txt_len, split_flag, tstep,
    )
    return velocity[None], moved[None]


def solution(mesh):
    rep = P()
    placed = (
        P(("group", "mp"), None), P("cfg", ("group", "mp"), None), rep,
        P(None, "mp"), P(None, "mp"),
    ) + (rep,) * 13
    out = P("cfg", ("group", "mp"), None)
    return jax.shard_map(
        local, mesh=mesh, in_specs=placed, out_specs=(out, out), check_vma=False
    )
```

```python
import functools
import math

import jax
import jax.numpy as jnp
from jax import lax
from jax.experimental import pallas as pl
from jax.experimental.pallas import tpu as pltpu
from jax.sharding import PartitionSpec as P

HD = 128
F32 = jnp.float32
BF16 = jnp.bfloat16
MESH = pl.DeviceIdType.MESH
TEXT_FROM = (0, 1, 3, 2)


def nt_dot(a, b):
    return lax.dot_general(a, b, (((1,), (1,)), ((), ())), preferred_element_type=F32)


def dot(a, b):
    return jnp.dot(a, b, preferred_element_type=F32)


def head_norm(values, gain):
    return values * lax.rsqrt(jnp.mean(values * values, -1, keepdims=True) + 1e-06) * gain


def split(values):
    high = values.astype(BF16)
    return high, (values - high.astype(F32)).astype(BF16)


def body(
    lat_h, text_h, win_h, wq_h, wt_h, wo_h, wf_h, mimg_h, mtxt_h, mfin_h,
    qg, kg, guide, step_size, img_len, txt_len, flags, tstep,
    vel_o, next_o,
    lat, text, win, wq, wt, wo, wf, mimg, mtxt, mfin,
    txt, lall, wx, lhs, rhs, bias, xc, q, kv, kvm, mask, maskm, acc, att,
    mix, mixr, fin, vsend, vrecv,
    lsem, ts, tr, ls, lr, ks, kr, ms, mr, vs, vr,
):
    c = lax.axis_index("cfg")
    g = lax.axis_index("group")
    m = lax.axis_index("mp")
    n_mp = 4
    right, left = lax.rem(m + 1, n_mp), lax.rem(m + 3, n_mp)
    mate = g + 1 - 2 * lax.rem(g, 2)
    ch, rows = lat_h.shape
    trows, d = text_h.shape
    heads = wq_h.shape[1] // (3 * HD)
    img, ntxt = rows * n_mp, trows * n_mp
    half = rows // 2
    part = trows // 4

    def chunk(i):
        return pl.ds(i * part, part)

    def local_copy(src, dst, i):
        copy = pltpu.make_async_copy(src, dst, lsem.at[i])
        copy.start()
        return copy

    c_text = {
        i: local_copy(text_h.at[chunk(i)], text.at[chunk(i)], 9 + heads + i) for i in (0, 2)
    }
    c_mtxt = local_copy(mtxt_h, mtxt, 1)
    c_lat = local_copy(lat_h, lat, 2)
    c_win = local_copy(win_h, win, 3)
    c_mimg = local_copy(mimg_h, mimg, 4)
    for i in (1, 3):
        c_text[i] = local_copy(text_h.at[chunk(i)], text.at[chunk(i)], 9 + heads + i)

    barrier = pltpu.get_barrier_semaphore()
    for k in (1, 2, 3):
        pl.semaphore_signal(
            barrier, inc=1, device_id={"mp": lax.rem(m + k, n_mp)}, device_id_type=MESH
        )
    pl.semaphore_signal(barrier, inc=1, device_id={"group": mate}, device_id_type=MESH)
    pl.semaphore_signal(barrier, inc=1, device_id={"cfg": 1 - c}, device_id_type=MESH)

    def remote(src, dst, ssem, rsem, device):
        return pltpu.make_async_remote_copy(
            src_ref=src, dst_ref=dst, send_sem=ssem, recv_sem=rsem,
            device_id=device, device_id_type=MESH,
        )

    step = tstep[g]
    il, tl = img_len[g], txt_len[g]
    il_m, tl_m = img_len[mate], txt_len[mate]
    flag = jnp.where(flags[c, g] == 1, 1.0, 0.0).astype(F32)

    to_right = [
        remote(txt.at[0, chunk(i)], txt.at[2, chunk(i)], ts.at[i], tr.at[i], {"mp": right})
        for i in range(4)
    ]
    to_left = [
        remote(txt.at[0, chunk(i)], txt.at[1, chunk(i)], ts.at[4 + i], tr.at[4 + i], {"mp": left})
        for i in range(4)
    ]
    on_right = [
        remote(txt.at[2, chunk(i)], txt.at[3, chunk(i)], ts.at[8 + i], tr.at[8 + i], {"mp": right})
        for i in (0, 1)
    ]
    on_left = [
        remote(txt.at[1, chunk(i)], txt.at[3, chunk(i)], ts.at[8 + i], tr.at[8 + i], {"mp": left})
        for i in (2, 3)
    ]

    def norm_text(i):
        x = text[chunk(i), :].astype(F32)
        center = x - jnp.mean(x, -1, keepdims=True)
        spread = jnp.mean(center * center, -1, keepdims=True)
        y = center * lax.rsqrt(spread + 1e-06) * (1.0 + mtxt[step, 1:2, :]) + mtxt[step, 0:1, :]
        txt[0, chunk(i), :] = y.astype(BF16)

    c_mtxt.wait()
    c_text[0].wait()
    norm_text(0)
    c_text[2].wait()
    norm_text(2)
    pl.semaphore_wait(barrier, 5)
    to_right[0].start()
    to_left[2].start()
    c_lat.wait()
    c_win.wait()
    c_mimg.wait()
    c_wq = [
        local_copy(wq_h.at[:, pl.ds(h * 3 * HD, 3 * HD)], wq.at[h], 5 + h) for h in range(heads)
    ]
    c_wt = local_copy(wt_h, wt, 5 + heads)

    e_row = lax.broadcasted_iota(jnp.int32, (ch, 2 * ch), 0)
    e_col = lax.broadcasted_iota(jnp.int32, (ch, 2 * ch), 1)
    twice = jnp.where((e_col == e_row) | (e_col == e_row + ch), 1.0, 0.0).astype(BF16)
    lat2 = lax.dot_general(
        lat[...].astype(BF16), twice, (((0,), (0,)), ((), ())), preferred_element_type=F32
    )
    w = win[...].astype(F32)
    w = w - jnp.mean(w, -1, keepdims=True)
    w_high, w_low = split(w)
    wx[0:ch, :] = w_high
    wx[ch : 2 * ch, :] = w_low
    lat2b = lat2.astype(BF16)
    squares = jnp.zeros((rows, HD), F32)
    wide = min(d, 512)
    for j in range(d // wide):
        x = dot(lat2b, wx[:, j * wide : (j + 1) * wide])
        xc[1 - c, :, j * wide : (j + 1) * wide] = x[0:half]
        xc[c, :, j * wide : (j + 1) * wide] = x[half:]
        for k in range(wide // HD):
            piece = x[:, k * HD : (k + 1) * HD]
            squares = squares + piece * piece
    rstd = lax.rsqrt(jnp.sum(squares, -1, keepdims=True) / d + 1e-06)
    scaled = lat2 * rstd
    scaled_high = scaled.astype(BF16).astype(F32)
    lane = lax.broadcasted_iota(jnp.int32, (rows, 2 * ch), 1)
    scaled = jnp.where(lane < ch, scaled_high, scaled - scaled_high).astype(BF16)
    lall[1 - c, 0] = scaled[0:half]
    lall[c, 0] = scaled[half:]
    lat_out = [
        remote(
            lall.at[:, 0], lall.at[:, 4 - k], ls.at[k - 1], lr.at[k - 1],
            {"mp": lax.rem(m + k, n_mp)},
        )
        for k in (1, 2, 3)
    ]
    for copy in lat_out:
        copy.start()

    c_text[1].wait()
    norm_text(1)
    c_text[3].wait()
    norm_text(3)
    to_right[1].start()
    to_left[3].start()
    to_right[2].start()
    to_left[0].start()
    to_right[3].start()
    to_left[1].start()
    c_wo = local_copy(wo_h, wo, 6 + heads)
    c_wf = local_copy(wf_h, wf, 7 + heads)
    c_mfin = local_copy(mfin_h, mfin, 8 + heads)

    s_high, s_low = split(w * (1.0 + mimg[1, pl.ds(step, 1), :]))
    lhs[0:ch, :] = s_high
    lhs[ch : 2 * ch, :] = s_low
    b_high, b_low = split(mimg[0, pl.ds(step, 1), :])
    b_row = lax.broadcasted_iota(jnp.int32, (16, d), 0)
    lhs[2 * ch :, :] = jnp.where(
        b_row == 0, b_high.astype(F32), jnp.where(b_row == 1, b_low.astype(F32), 0.0)
    ).astype(BF16)

    def fill_mask(ref, img_live, txt_live, on):
        spot = lax.broadcasted_iota(jnp.int32, (half, HD), 0)
        for side in range(2):
            place = (1 - c) if side == 0 else c
            for k in range(4):
                start = lax.rem(m + k, n_mp) * rows + place * half
                at = side * 4 * half + k * half
                ref[at : at + half, :] = jnp.where(spot + start < img_live, on, 0.0).astype(BF16)
        spot_t = lax.broadcasted_iota(jnp.int32, (trows, HD), 0)
        for k in range(4):
            start = lax.rem(m + TEXT_FROM[k], n_mp) * trows
            ref[img + k * trows : img + (k + 1) * trows, :] = jnp.where(
                spot_t + start < txt_live, on, 0.0
            ).astype(BF16)

    fill_mask(mask, il, tl, 1.0)
    fill_mask(maskm, il_m, tl_m, flag)

    for h in range(heads):
        c_wq[h].wait()
        full = dot(lhs[...], wq[h])
        fold = full[0:ch] + full[ch : 2 * ch]
        high, low = split(fold)
        rhs[h, 0:ch, :] = high
        rhs[h, ch : 2 * ch, :] = high
        rhs[h, 2 * ch : 3 * ch, :] = low
        rhs[h, 3 * ch : 4 * ch, :] = low
        bias[h] = full[2 * ch : 2 * ch + 8]
    for copy in lat_out:
        copy.wait_recv()
    q_gain = qg[...] * (HD ** (-0.5) * math.log2(math.e))
    k_gain = kg[...]
    block_rows = 4 * half

    def image_block(side, carry):
        block = jnp.concatenate([lall[side, k] for k in range(4)], axis=0)
        block = jnp.concatenate([block, block], axis=1)
        at = pl.ds(pl.multiple_of(side * block_rows, block_rows), block_rows)
        for h in range(heads):
            x = dot(block, rhs[h]) + (bias[h, 0:1, :] + bias[h, 1:2, :])
            q[h, at, :] = head_norm(x[:, 0:HD], q_gain).astype(BF16)
            kv[h, at, 0:HD] = head_norm(x[:, HD : 2 * HD], k_gain).astype(BF16)
            kv[h, at, HD : 2 * HD] = x[:, 2 * HD :].astype(BF16) * mask[at, :]
        return carry

    lax.fori_loop(0, 2, image_block, 0)
    kv_img = [
        remote(
            kv.at[h, pl.ds(0, img)], kvm.at[h, pl.ds(0, img)], ks.at[h], kr.at[h],
            {"group": mate},
        )
        for h in range(heads)
    ]
    for copy in kv_img:
        copy.start()

    def text_block(first, count):
        span = slice(img + first * trows, img + (first + count) * trows)
        lhs_t = txt[first] if count == 1 else jnp.concatenate(
            [txt[first + k] for k in range(count)], axis=0
        )
        copies = []
        for h in range(heads):
            x = dot(lhs_t, wt[:, h * 2 * HD : (h + 1) * 2 * HD])
            kv[h, span, 0:HD] = head_norm(x[:, 0:HD], k_gain).astype(BF16)
            kv[h, span, HD : 2 * HD] = x[:, HD:].astype(BF16) * mask[span, :]
            i = heads + (first if first < 2 else 2) * heads + h
            rows_t = pl.ds(img + first * trows, count * trows)
            copy = remote(
                kv.at[h, rows_t], kvm.at[h, rows_t], ks.at[i], kr.at[i], {"group": mate}
            )
            copy.start()
            copies.append(copy)
        return copies

    c_wt.wait()
    kv_txt = text_block(0, 1)
    on = flag.astype(BF16)

    def keys(h, parts):
        return jnp.concatenate([ref[h, lo : lo + n, 0:HD] for ref, lo, n in parts], axis=0)

    def values(h, parts):
        rows_v = []
        for ref, lo, n in parts:
            v = ref[h, lo : lo + n, HD : 2 * HD]
            if ref is kvm:
                v = v * on
            live = (maskm if ref is kvm else mask)[lo : lo + n, :]
            rows_v.append(jnp.concatenate([v, live], axis=1))
        return jnp.concatenate(rows_v, axis=0)

    def attend(h, at, parts):
        p = jnp.exp2(nt_dot(q[h, at, :], keys(h, parts))).astype(BF16)
        return dot(p, values(h, parts))

    def each_side(fn):
        def run(side, carry):
            at = pl.ds(pl.multiple_of(side * block_rows, block_rows), block_rows)
            for h in range(heads):
                fn(h, at)
            return carry

        lax.fori_loop(0, 2, run, 0)

    def own_image(h, at):
        acc[h, at, :] = attend(h, at, [(kv, 0, img)])

    each_side(own_image)

    to_right[0].wait_recv()
    on_right[0].start()
    to_left[2].wait_recv()
    on_left[0].start()
    for copy in kv_img:
        copy.wait_recv()

    def mate_image(h, at):
        acc[h, at, :] += attend(h, at, [(kvm, 0, img)])

    each_side(mate_image)

    to_right[1].wait_recv()
    on_right[1].start()
    to_left[3].wait_recv()
    on_left[1].start()
    to_right[2].wait_recv()
    to_right[3].wait_recv()
    to_left[0].wait_recv()
    to_left[1].wait_recv()
    kv_txt += text_block(1, 2)
    for copy in kv_txt:
        copy.wait_recv()

    def most_text(h, at):
        acc[h, at, :] += attend(h, at, [(kv, img, 3 * trows), (kvm, img, 3 * trows)])

    each_side(most_text)

    for copy in on_right + on_left:
        copy.wait_recv()
    kv_last = text_block(3, 1)
    last = img + 3 * trows

    mixes = []
    for side in range(2):
        for h in range(heads):
            if side == 0:
                kv_last[h].wait_recv()
            at = slice(side * block_rows, (side + 1) * block_rows)
            total = acc[h, at, :] + attend(h, at, [(kv, last, trows), (kvm, last, trows)])
            share = (total[:, 0:HD] / total[:, HD : 2 * HD]).astype(BF16)
            for k in range(4):
                mix[side, k, h] = share[k * half : (k + 1) * half]
        copies = {}
        for k in (2, 1, 3):
            i = side * 3 + k - 1
            copies[k] = remote(
                mix.at[side, k], mixr.at[side, 3 - k], ms.at[i], mr.at[i],
                {"mp": lax.rem(m + k, n_mp)},
            )
            copies[k].start()
        mixes.append(copies)

    def project(side, ref, k, first):
        base = pl.multiple_of(lax.rem(m + k, n_mp) * (heads * HD), heads * HD)
        own = jnp.concatenate([ref[h] for h in range(heads)], axis=1)
        for j in range(d // wide):
            cols = slice(j * wide, (j + 1) * wide)
            x = dot(own, wo[pl.ds(base, heads * HD), cols])
            att[side, :, cols] = x if first else att[side, :, cols] + x

    def finish(side):
        small = min(half, 32)
        for i in range(half // small):
            at = slice(i * small, (i + 1) * small)
            x = xc[side, at, :] + mimg[2, pl.ds(step, 1), :] * att[side, at, :]
            center = x - jnp.mean(x, -1, keepdims=True)
            spread = jnp.mean(center * center, -1, keepdims=True)
            y = center * lax.rsqrt(spread + 1e-06) * (1.0 + mfin[step, 1:2, :]) + mfin[step, 0:1, :]
            fin[at, :] = y.astype(BF16)
        return nt_dot(wf[...], fin[...])

    c_wo.wait()
    project(0, mix.at[0, 0], 0, True)
    project(1, mix.at[1, 0], 0, True)
    c_wf.wait()
    c_mfin.wait()
    for k in (2, 1, 3):
        mixes[0][k].wait_recv()
        project(0, mixr.at[0, 3 - k], 4 - k, False)
    vsend[...] = finish(0)
    swap = remote(vsend, vrecv, vs.at[0], vr.at[0], {"cfg": 1 - c})
    swap.start()
    for k in (2, 1, 3):
        mixes[1][k].wait_recv()
        project(1, mixr.at[1, 3 - k], 4 - k, False)
    own = finish(1)
    swap.wait_recv()
    other = vrecv[...]
    cond = jnp.where(c == 0, own, other)
    uncond = jnp.where(c == 0, other, own)
    guided = uncond + guide[g] * (cond - uncond)
    spot = lax.broadcasted_iota(jnp.int32, (ch, half), 1) + (m * rows + c * half)
    guided = jnp.where(spot < il, guided, 0.0)
    vel_o[...] = guided
    next_o[...] = lat[:, pl.ds(pl.multiple_of(c * half, half), half)] - step_size[step] * guided

    for copy in to_right + to_left + on_right + on_left + lat_out + kv_img + kv_txt + kv_last:
        copy.wait_send()
    for copies in mixes:
        for k in (2, 1, 3):
            copies[k].wait_send()
    swap.wait_send()


def local(
    latents, text_hidden, w_img_in, w_img_qkv, w_txt_kv, q_gain, k_gain, w_out, w_final,
    mod_img, mod_txt, mod_final, guide, step_size, img_len, txt_len, split_flag, tstep,
):
    text = text_hidden[0]
    rows, ch = latents.shape
    trows, d = text.shape
    heads = w_img_qkv.shape[1] // (3 * HD)
    img, ntxt = 4 * rows, 4 * trows
    half = rows // 2
    hbm = pl.BlockSpec(memory_space=pl.ANY)
    vmem = pl.BlockSpec(memory_space=pltpu.VMEM)
    smem = pl.BlockSpec(memory_space=pltpu.SMEM)
    dma = pltpu.SemaphoreType.DMA
    out = jax.ShapeDtypeStruct((ch, half), F32)
    scratch = [
        pltpu.VMEM((ch, rows), F32),
        pltpu.VMEM(text.shape, BF16),
        pltpu.VMEM(w_img_in.shape, BF16),
        pltpu.VMEM((heads, d, 3 * HD), BF16),
        pltpu.VMEM(w_txt_kv.shape, BF16),
        pltpu.VMEM(w_out.shape, BF16),
        pltpu.VMEM((ch, d), BF16),
        pltpu.VMEM((3, mod_img.shape[0], d), F32),
        pltpu.VMEM(mod_txt.shape, F32),
        pltpu.VMEM(mod_final.shape, F32),
        pltpu.VMEM((4, trows, d), BF16),
        pltpu.VMEM((2, 4, half, 2 * ch), BF16),
        pltpu.VMEM((2 * ch, d), BF16),
        pltpu.VMEM((2 * ch + 16, d), BF16),
        pltpu.VMEM((heads, 4 * ch, 3 * HD), BF16),
        pltpu.VMEM((heads, 8, 3 * HD), F32),
        pltpu.VMEM((2, half, d), F32),
        pltpu.VMEM((heads, img, HD), BF16),
        pltpu.VMEM((heads, img + ntxt, 2 * HD), BF16),
        pltpu.VMEM((heads, img + ntxt, 2 * HD), BF16),
        pltpu.VMEM((img + ntxt, HD), BF16),
        pltpu.VMEM((img + ntxt, HD), BF16),
        pltpu.VMEM((heads, img, 2 * HD), F32),
        pltpu.VMEM((2, half, d), F32),
        pltpu.VMEM((2, 4, heads, half, HD), BF16),
        pltpu.VMEM((2, 3, heads, half, HD), BF16),
        pltpu.VMEM((half, d), BF16),
        pltpu.VMEM((ch, half), F32),
        pltpu.VMEM((ch, half), F32),
        dma((13 + heads,)),
        dma((12,)), dma((12,)),
        dma((3,)), dma((3,)),
        dma((4 * heads,)), dma((4 * heads,)),
        dma((6,)), dma((6,)),
        dma((1,)), dma((1,)),
    ]
    velocity, moved = pl.pallas_call(
        body,
        out_shape=(out, out),
        in_specs=[hbm] * 10 + [vmem] * 2 + [smem] * 6,
        out_specs=(vmem, vmem),
        scratch_shapes=scratch,
        compiler_params=pltpu.CompilerParams(
            collective_id=0, has_side_effects=True, vmem_limit_bytes=61 * 1024 * 1024
        ),
        name="guided_step",
    )(
        latents.T, text, w_img_in, w_img_qkv, w_txt_kv, w_out, w_final.T,
        jnp.transpose(mod_img, (1, 0, 2)), mod_txt, mod_final,
        q_gain[None], k_gain[None], guide, step_size, img_len, txt_len, split_flag, tstep,
    )
    return velocity.T[None], moved.T[None]


def solution(mesh):
    rep = P()
    placed = (
        P(("group", "mp"), None), P("cfg", ("group", "mp"), None), rep,
        P(None, "mp"), P(None, "mp"),
    ) + (rep,) * 13
    out = P("cfg", ("group", "mp"), None)
    return jax.shard_map(
        local, mesh=mesh, in_specs=placed, out_specs=(out, out), check_vma=False
    )
```

```python
import functools
import math

import jax
import jax.numpy as jnp
from jax import lax
from jax.experimental import pallas as pl
from jax.experimental.pallas import tpu as pltpu
from jax.sharding import PartitionSpec as P

HD = 128
F32 = jnp.float32
BF16 = jnp.bfloat16
MESH = pl.DeviceIdType.MESH
TEXT_FROM = (0, 1, 3, 2)


def nt_dot(a, b):
    return lax.dot_general(a, b, (((1,), (1,)), ((), ())), preferred_element_type=F32)


def dot(a, b):
    return jnp.dot(a, b, preferred_element_type=F32)


def head_norm(values, gain):
    return values * lax.rsqrt(jnp.mean(values * values, -1, keepdims=True) + 1e-06) * gain


def split(values):
    high = values.astype(BF16)
    return high, (values - high.astype(F32)).astype(BF16)


def body(
    lat_h, text_h, win_h, wq_h, wt_h, wo_h, wf_h, mimg_h, mtxt_h, mfin_h,
    qg, kg, guide, step_size, img_len, txt_len, flags, tstep,
    out,
    lat, text, win, wq, wt, wo, wf, mimg, mtxt, mfin,
    txt, lall, wx, lhs, rhs, bias, xc, q, kv, kvm, mask, maskm, acc, att,
    mix, mixr, fin, vsend, vrecv,
    lsem, ts, tr, ls, lr, ks, kr, ms, mr, vs, vr,
):
    c = lax.axis_index("cfg")
    g = lax.axis_index("group")
    m = lax.axis_index("mp")
    n_mp = 4
    right, left = lax.rem(m + 1, n_mp), lax.rem(m + 3, n_mp)
    mate = g + 1 - 2 * lax.rem(g, 2)
    ch, rows = lat_h.shape
    trows, d = text_h.shape
    heads = wq_h.shape[1] // (3 * HD)
    img, ntxt = rows * n_mp, trows * n_mp
    half = rows // 2
    part = trows // 4

    def chunk(i):
        return pl.ds(i * part, part)

    def local_copy(src, dst, i):
        copy = pltpu.make_async_copy(src, dst, lsem.at[i])
        copy.start()
        return copy

    c_lat = local_copy(lat_h, lat, 2)
    c_win = local_copy(win_h, win, 3)
    c_mtxt = local_copy(mtxt_h, mtxt, 1)
    c_text = local_copy(text_h, text, 0)
    c_mimg = local_copy(mimg_h, mimg, 4)

    barrier = pltpu.get_barrier_semaphore()
    for k in (1, 2, 3):
        pl.semaphore_signal(
            barrier, inc=1, device_id={"mp": lax.rem(m + k, n_mp)}, device_id_type=MESH
        )
    pl.semaphore_signal(barrier, inc=1, device_id={"group": mate}, device_id_type=MESH)
    pl.semaphore_signal(barrier, inc=1, device_id={"cfg": 1 - c}, device_id_type=MESH)

    def remote(src, dst, ssem, rsem, device):
        return pltpu.make_async_remote_copy(
            src_ref=src, dst_ref=dst, send_sem=ssem, recv_sem=rsem,
            device_id=device, device_id_type=MESH,
        )

    step = tstep[g]
    il, tl = img_len[g], txt_len[g]
    il_m, tl_m = img_len[mate], txt_len[mate]
    flag = jnp.where(flags[c, g] == 1, 1.0, 0.0).astype(F32)

    def source(i, first):
        return text_h.at[chunk(i)] if i == first else txt.at[0, chunk(i)]

    to_right = [
        remote(source(i, 0), txt.at[2, chunk(i)], ts.at[i], tr.at[i], {"mp": right})
        for i in range(4)
    ]
    to_left = [
        remote(source(i, 2), txt.at[1, chunk(i)], ts.at[4 + i], tr.at[4 + i], {"mp": left})
        for i in range(4)
    ]
    on_right = [
        remote(txt.at[2, chunk(i)], txt.at[3, chunk(i)], ts.at[8 + i], tr.at[8 + i], {"mp": right})
        for i in (0, 1)
    ]
    on_left = [
        remote(txt.at[1, chunk(i)], txt.at[3, chunk(i)], ts.at[8 + i], tr.at[8 + i], {"mp": left})
        for i in (2, 3)
    ]

    def norm_text(i, slot=0):
        x = (text[chunk(i), :] if slot == 0 else txt[slot, chunk(i), :]).astype(F32)
        center = x - jnp.mean(x, -1, keepdims=True)
        spread = jnp.mean(center * center, -1, keepdims=True)
        y = center * lax.rsqrt(spread + 1e-06) * (1.0 + mtxt[step, 1:2, :]) + mtxt[step, 0:1, :]
        txt[slot, chunk(i), :] = y.astype(BF16)

    pl.semaphore_wait(barrier, 5)
    to_right[0].start()
    to_left[2].start()
    c_lat.wait()
    c_win.wait()

    e_row = lax.broadcasted_iota(jnp.int32, (ch, 2 * ch), 0)
    e_col = lax.broadcasted_iota(jnp.int32, (ch, 2 * ch), 1)
    twice = jnp.where((e_col == e_row) | (e_col == e_row + ch), 1.0, 0.0).astype(BF16)
    lat2 = lax.dot_general(
        lat[...].astype(BF16), twice, (((0,), (0,)), ((), ())), preferred_element_type=F32
    )
    w = win[...].astype(F32)
    w = w - jnp.mean(w, -1, keepdims=True)
    w_high, w_low = split(w)
    wx[0:ch, :] = w_high
    wx[ch : 2 * ch, :] = w_low
    lat2b = lat2.astype(BF16)
    squares = jnp.zeros((rows, HD), F32)
    wide = min(d, 512)
    for j in range(d // wide):
        x = dot(lat2b, wx[:, j * wide : (j + 1) * wide])
        xc[1 - c, :, j * wide : (j + 1) * wide] = x[0:half]
        xc[c, :, j * wide : (j + 1) * wide] = x[half:]
        for k in range(wide // HD):
            piece = x[:, k * HD : (k + 1) * HD]
            squares = squares + piece * piece
    rstd = lax.rsqrt(jnp.sum(squares, -1, keepdims=True) / d + 1e-06)
    scaled = lat2 * rstd
    scaled_high = scaled.astype(BF16).astype(F32)
    lane = lax.broadcasted_iota(jnp.int32, (rows, 2 * ch), 1)
    scaled = jnp.where(lane < ch, scaled_high, scaled - scaled_high).astype(BF16)
    lall[1 - c, 0] = scaled[0:half]
    lall[c, 0] = scaled[half:]
    lat_out = [
        remote(
            lall.at[:, 0], lall.at[:, 4 - k], ls.at[k - 1], lr.at[k - 1],
            {"mp": lax.rem(m + k, n_mp)},
        )
        for k in (1, 2, 3)
    ]
    for copy in lat_out:
        copy.start()

    c_mtxt.wait()
    c_text.wait()
    c_mimg.wait()
    c_wq = [
        local_copy(wq_h.at[:, pl.ds(h * 3 * HD, 3 * HD)], wq.at[h], 5 + h) for h in range(heads)
    ]
    c_wt = local_copy(wt_h, wt, 5 + heads)
    norm_text(1)
    to_right[1].start()
    norm_text(3)
    to_left[3].start()
    norm_text(2)
    to_right[2].start()
    norm_text(0)
    to_left[0].start()
    to_right[3].start()
    to_left[1].start()
    c_wo = local_copy(wo_h, wo, 6 + heads)
    c_wf = local_copy(wf_h, wf, 7 + heads)
    c_mfin = local_copy(mfin_h, mfin, 8 + heads)

    s_high, s_low = split(w * (1.0 + mimg[1, pl.ds(step, 1), :]))
    lhs[0:ch, :] = s_high
    lhs[ch : 2 * ch, :] = s_low
    b_high, b_low = split(mimg[0, pl.ds(step, 1), :])
    b_row = lax.broadcasted_iota(jnp.int32, (16, d), 0)
    lhs[2 * ch :, :] = jnp.where(
        b_row == 0, b_high.astype(F32), jnp.where(b_row == 1, b_low.astype(F32), 0.0)
    ).astype(BF16)

    def fill_mask(ref, img_live, txt_live, on):
        spot = lax.broadcasted_iota(jnp.int32, (half, HD), 0)
        for side in range(2):
            place = (1 - c) if side == 0 else c
            for k in range(4):
                start = lax.rem(m + k, n_mp) * rows + place * half
                at = side * 4 * half + k * half
                ref[at : at + half, :] = jnp.where(spot + start < img_live, on, 0.0).astype(BF16)
        spot_t = lax.broadcasted_iota(jnp.int32, (trows, HD), 0)
        for k in range(4):
            start = lax.rem(m + TEXT_FROM[k], n_mp) * trows
            ref[img + k * trows : img + (k + 1) * trows, :] = jnp.where(
                spot_t + start < txt_live, on, 0.0
            ).astype(BF16)

    fill_mask(mask, il, tl, 1.0)
    fill_mask(maskm, il_m, tl_m, flag)

    for h in range(heads):
        c_wq[h].wait()
        full = dot(lhs[...], wq[h])
        fold = full[0:ch] + full[ch : 2 * ch]
        high, low = split(fold)
        rhs[h, 0:ch, :] = high
        rhs[h, ch : 2 * ch, :] = high
        rhs[h, 2 * ch : 3 * ch, :] = low
        rhs[h, 3 * ch : 4 * ch, :] = low
        bias[h] = full[2 * ch : 2 * ch + 8]
    for copy in lat_out:
        copy.wait_recv()
    q_gain = qg[...] * (HD ** (-0.5) * math.log2(math.e))
    k_gain = kg[...]
    block_rows = 4 * half

    def image_block(side, carry):
        block = jnp.concatenate([lall[side, k] for k in range(4)], axis=0)
        block = jnp.concatenate([block, block], axis=1)
        at = pl.ds(pl.multiple_of(side * block_rows, block_rows), block_rows)
        for h in range(heads):
            x = dot(block, rhs[h]) + (bias[h, 0:1, :] + bias[h, 1:2, :])
            q[h, at, :] = head_norm(x[:, 0:HD], q_gain).astype(BF16)
            kv[h, at, 0:HD] = head_norm(x[:, HD : 2 * HD], k_gain).astype(BF16)
            kv[h, at, HD : 2 * HD] = x[:, 2 * HD :].astype(BF16) * mask[at, :]
        return carry

    lax.fori_loop(0, 2, image_block, 0)
    kv_img = [
        remote(
            kv.at[h, pl.ds(0, img)], kvm.at[h, pl.ds(0, img)], ks.at[h], kr.at[h],
            {"group": mate},
        )
        for h in range(heads)
    ]
    for copy in kv_img:
        copy.start()

    def text_block(first, count):
        span = slice(img + first * trows, img + (first + count) * trows)
        lhs_t = txt[first] if count == 1 else jnp.concatenate(
            [txt[first + k] for k in range(count)], axis=0
        )
        copies = []
        for h in range(heads):
            x = dot(lhs_t, wt[:, h * 2 * HD : (h + 1) * 2 * HD])
            kv[h, span, 0:HD] = head_norm(x[:, 0:HD], k_gain).astype(BF16)
            kv[h, span, HD : 2 * HD] = x[:, HD:].astype(BF16) * mask[span, :]
            i = heads + (first if first < 2 else 2) * heads + h
            rows_t = pl.ds(img + first * trows, count * trows)
            copy = remote(
                kv.at[h, rows_t], kvm.at[h, rows_t], ks.at[i], kr.at[i], {"group": mate}
            )
            copy.start()
            copies.append(copy)
        return copies

    c_wt.wait()
    kv_txt = text_block(0, 1)
    on = flag.astype(BF16)

    def keys(h, parts):
        return jnp.concatenate([ref[h, lo : lo + n, 0:HD] for ref, lo, n in parts], axis=0)

    def values(h, parts):
        rows_v = []
        for ref, lo, n in parts:
            v = ref[h, lo : lo + n, HD : 2 * HD]
            if ref is kvm:
                v = v * on
            live = (maskm if ref is kvm else mask)[lo : lo + n, :]
            rows_v.append(jnp.concatenate([v, live], axis=1))
        return jnp.concatenate(rows_v, axis=0)

    def attend(h, at, parts):
        p = jnp.exp2(nt_dot(q[h, at, :], keys(h, parts))).astype(BF16)
        return dot(p, values(h, parts))

    def each_side(fn):
        def run(side, carry):
            at = pl.ds(pl.multiple_of(side * block_rows, block_rows), block_rows)
            for h in range(heads):
                fn(h, at)
            return carry

        lax.fori_loop(0, 2, run, 0)

    def own_image(h, at):
        acc[h, at, :] = attend(h, at, [(kv, 0, img)])

    each_side(own_image)

    to_right[0].wait_recv()
    norm_text(0, slot=2)
    on_right[0].start()
    to_left[2].wait_recv()
    norm_text(2, slot=1)
    on_left[0].start()
    for copy in kv_img:
        copy.wait_recv()

    def mate_image(h, at):
        acc[h, at, :] += attend(h, at, [(kvm, 0, img)])

    each_side(mate_image)

    to_right[1].wait_recv()
    on_right[1].start()
    to_left[3].wait_recv()
    on_left[1].start()
    to_right[2].wait_recv()
    to_right[3].wait_recv()
    to_left[0].wait_recv()
    to_left[1].wait_recv()
    kv_txt += text_block(1, 2)
    for copy in kv_txt:
        copy.wait_recv()

    def most_text(h, at):
        acc[h, at, :] += attend(h, at, [(kv, img, 3 * trows), (kvm, img, 3 * trows)])

    each_side(most_text)

    for copy in on_right + on_left:
        copy.wait_recv()
    kv_last = text_block(3, 1)
    last = img + 3 * trows

    mixes = []
    for side in range(2):
        copies = {k: [] for k in (1, 2, 3)}
        for h in range(heads):
            if side == 0:
                kv_last[h].wait_recv()
            at = slice(side * block_rows, (side + 1) * block_rows)
            total = acc[h, at, :] + attend(h, at, [(kv, last, trows), (kvm, last, trows)])
            share = (total[:, 0:HD] / total[:, HD : 2 * HD]).astype(BF16)
            for k in range(4):
                mix[side, k, h] = share[k * half : (k + 1) * half]
            for k in (2, 1, 3):
                i = (side * 3 + k - 1) * heads + h
                copy = remote(
                    mix.at[side, k, h], mixr.at[side, 3 - k, h], ms.at[i], mr.at[i],
                    {"mp": lax.rem(m + k, n_mp)},
                )
                copy.start()
                copies[k].append(copy)
        mixes.append(copies)

    def project(side, ref, k, first):
        base = pl.multiple_of(lax.rem(m + k, n_mp) * (heads * HD), heads * HD)
        own = jnp.concatenate([ref[h] for h in range(heads)], axis=1)
        for j in range(d // wide):
            cols = slice(j * wide, (j + 1) * wide)
            x = dot(own, wo[pl.ds(base, heads * HD), cols])
            att[side, :, cols] = x if first else att[side, :, cols] + x

    def finish(side):
        small = min(half, 32)
        for i in range(half // small):
            at = slice(i * small, (i + 1) * small)
            x = xc[side, at, :] + mimg[2, pl.ds(step, 1), :] * att[side, at, :]
            center = x - jnp.mean(x, -1, keepdims=True)
            spread = jnp.mean(center * center, -1, keepdims=True)
            y = center * lax.rsqrt(spread + 1e-06) * (1.0 + mfin[step, 1:2, :]) + mfin[step, 0:1, :]
            fin[at, :] = y.astype(BF16)
        return nt_dot(wf[...], fin[...])

    c_wo.wait()
    project(0, mix.at[0, 0], 0, True)
    project(1, mix.at[1, 0], 0, True)
    c_wf.wait()
    c_mfin.wait()
    for k in (1, 3, 2):
        for copy in mixes[0][k]:
            copy.wait_recv()
        project(0, mixr.at[0, 3 - k], 4 - k, False)
    vsend[...] = finish(0)
    swap = remote(vsend, vrecv, vs.at[0], vr.at[0], {"cfg": 1 - c})
    swap.start()
    for k in (1, 3, 2):
        for copy in mixes[1][k]:
            copy.wait_recv()
        project(1, mixr.at[1, 3 - k], 4 - k, False)
    own = finish(1)
    swap.wait_recv()
    other = vrecv[...]
    cond = jnp.where(c == 0, own, other)
    uncond = jnp.where(c == 0, other, own)
    guided = uncond + guide[g] * (cond - uncond)
    spot = lax.broadcasted_iota(jnp.int32, (ch, half), 1) + (m * rows + c * half)
    guided = jnp.where(spot < il, guided, 0.0)
    out[0] = guided
    out[1] = lat[:, pl.ds(pl.multiple_of(c * half, half), half)] - step_size[step] * guided

    for copy in to_right + to_left + on_right + on_left + lat_out + kv_img + kv_txt + kv_last:
        copy.wait_send()
    for copies in mixes:
        for k in (2, 1, 3):
            for copy in copies[k]:
                copy.wait_send()
    swap.wait_send()


def unpack(both, velocity, moved, sem):
    copies = [
        pltpu.make_async_copy(both.at[i], ref, sem.at[i]) for i, ref in enumerate((velocity, moved))
    ]
    for copy in copies:
        copy.start()
    for copy in copies:
        copy.wait()


def local(
    latents, text_hidden, w_img_in, w_img_qkv, w_txt_kv, q_gain, k_gain, w_out, w_final,
    mod_img, mod_txt, mod_final, guide, step_size, img_len, txt_len, split_flag, tstep,
):
    text = text_hidden[0]
    rows, ch = latents.shape
    trows, d = text.shape
    heads = w_img_qkv.shape[1] // (3 * HD)
    img, ntxt = 4 * rows, 4 * trows
    half = rows // 2
    hbm = pl.BlockSpec(memory_space=pl.ANY)
    vmem = pl.BlockSpec(memory_space=pltpu.VMEM)
    smem = pl.BlockSpec(memory_space=pltpu.SMEM)
    dma = pltpu.SemaphoreType.DMA
    out = jax.ShapeDtypeStruct((2, ch, half), F32)
    single = jax.ShapeDtypeStruct((ch, half), F32)
    scratch = [
        pltpu.VMEM((ch, rows), F32),
        pltpu.VMEM(text.shape, BF16),
        pltpu.VMEM(w_img_in.shape, BF16),
        pltpu.VMEM((heads, d, 3 * HD), BF16),
        pltpu.VMEM(w_txt_kv.shape, BF16),
        pltpu.VMEM(w_out.shape, BF16),
        pltpu.VMEM((ch, d), BF16),
        pltpu.VMEM((3, mod_img.shape[0], d), F32),
        pltpu.VMEM(mod_txt.shape, F32),
        pltpu.VMEM(mod_final.shape, F32),
        pltpu.VMEM((4, trows, d), BF16),
        pltpu.VMEM((2, 4, half, 2 * ch), BF16),
        pltpu.VMEM((2 * ch, d), BF16),
        pltpu.VMEM((2 * ch + 16, d), BF16),
        pltpu.VMEM((heads, 4 * ch, 3 * HD), BF16),
        pltpu.VMEM((heads, 8, 3 * HD), F32),
        pltpu.VMEM((2, half, d), F32),
        pltpu.VMEM((heads, img, HD), BF16),
        pltpu.VMEM((heads, img + ntxt, 2 * HD), BF16),
        pltpu.VMEM((heads, img + ntxt, 2 * HD), BF16),
        pltpu.VMEM((img + ntxt, HD), BF16),
        pltpu.VMEM((img + ntxt, HD), BF16),
        pltpu.VMEM((heads, img, 2 * HD), F32),
        pltpu.VMEM((2, half, d), F32),
        pltpu.VMEM((2, 4, heads, half, HD), BF16),
        pltpu.VMEM((2, 3, heads, half, HD), BF16),
        pltpu.VMEM((half, d), BF16),
        pltpu.VMEM((ch, half), F32),
        pltpu.VMEM((ch, half), F32),
        dma((13 + heads,)),
        dma((12,)), dma((12,)),
        dma((3,)), dma((3,)),
        dma((4 * heads,)), dma((4 * heads,)),
        dma((6 * heads,)), dma((6 * heads,)),
        dma((1,)), dma((1,)),
    ]
    both = pl.pallas_call(
        body,
        out_shape=out,
        in_specs=[hbm] * 10 + [vmem] * 2 + [smem] * 6,
        out_specs=vmem,
        scratch_shapes=scratch,
        compiler_params=pltpu.CompilerParams(
            collective_id=0, has_side_effects=True, vmem_limit_bytes=61 * 1024 * 1024
        ),
        name="guided_step",
    )(
        latents.T, text, w_img_in, w_img_qkv, w_txt_kv, w_out, w_final.T,
        jnp.transpose(mod_img, (1, 0, 2)), mod_txt, mod_final,
        q_gain[None], k_gain[None], guide, step_size, img_len, txt_len, split_flag, tstep,
    )
    velocity, moved = pl.pallas_call(
        unpack,
        out_shape=(single, single),
        in_specs=[hbm],
        out_specs=(hbm, hbm),
        scratch_shapes=[dma((2,))],
        name="unpack",
    )(both)
    return velocity.T[None], moved.T[None]


def solution(mesh):
    rep = P()
    placed = (
        P(("group", "mp"), None), P("cfg", ("group", "mp"), None), rep,
        P(None, "mp"), P(None, "mp"),
    ) + (rep,) * 13
    out = P("cfg", ("group", "mp"), None)
    return jax.shard_map(
        local, mesh=mesh, in_specs=placed, out_specs=(out, out), check_vma=False
    )
```

```python
import functools
import math

import jax
import jax.numpy as jnp
from jax import lax
from jax.experimental import pallas as pl
from jax.experimental.pallas import tpu as pltpu
from jax.sharding import PartitionSpec as P

HD = 128
F32 = jnp.float32
BF16 = jnp.bfloat16
MESH = pl.DeviceIdType.MESH
TEXT_FROM = (0, 1, 3, 2)


def nt_dot(a, b):
    return lax.dot_general(a, b, (((1,), (1,)), ((), ())), preferred_element_type=F32)


def dot(a, b):
    return jnp.dot(a, b, preferred_element_type=F32)


def head_norm(values, gain):
    return values * lax.rsqrt(jnp.mean(values * values, -1, keepdims=True) + 1e-06) * gain


def split(values):
    high = values.astype(BF16)
    return high, (values - high.astype(F32)).astype(BF16)


def body(
    lat_h, text_h, win_h, wq_h, wt_h, wo_h, wf_h, mimg_h, mtxt_h, mfin_h,
    qg, kg, guide, step_size, img_len, txt_len, flags, tstep,
    out,
    lat, text, win, wq, wt, wo, wf, mimg, mtxt, mfin,
    txt, lall, wx, lhs, rhs, bias, xc, q, kv, kvm, mask, maskm, acc, att,
    mix, mixr, fin, vsend, vrecv,
    lsem, ts, tr, ls, lr, ks, kr, ms, mr, vs, vr,
):
    c = lax.axis_index("cfg")
    g = lax.axis_index("group")
    m = lax.axis_index("mp")
    n_mp = 4
    right, left = lax.rem(m + 1, n_mp), lax.rem(m + 3, n_mp)
    mate = g + 1 - 2 * lax.rem(g, 2)
    ch, rows = lat_h.shape
    trows, d = text_h.shape
    heads = wq_h.shape[1] // (3 * HD)
    img, ntxt = rows * n_mp, trows * n_mp
    half = rows // 2
    part = trows // 4

    def chunk(i):
        return pl.ds(i * part, part)

    def local_copy(src, dst, i):
        copy = pltpu.make_async_copy(src, dst, lsem.at[i])
        copy.start()
        return copy

    c_lat = local_copy(lat_h, lat, 2)
    c_win = local_copy(win_h, win, 3)
    c_mtxt = local_copy(mtxt_h, mtxt, 1)
    c_text = local_copy(text_h, text, 0)
    c_mimg = local_copy(mimg_h, mimg, 4)

    barrier = pltpu.get_barrier_semaphore()
    for k in (1, 2, 3):
        pl.semaphore_signal(
            barrier, inc=1, device_id={"mp": lax.rem(m + k, n_mp)}, device_id_type=MESH
        )
    pl.semaphore_signal(barrier, inc=1, device_id={"group": mate}, device_id_type=MESH)
    pl.semaphore_signal(barrier, inc=1, device_id={"cfg": 1 - c}, device_id_type=MESH)

    def remote(src, dst, ssem, rsem, device):
        return pltpu.make_async_remote_copy(
            src_ref=src, dst_ref=dst, send_sem=ssem, recv_sem=rsem,
            device_id=device, device_id_type=MESH,
        )

    step = tstep[g]
    il, tl = img_len[g], txt_len[g]
    il_m, tl_m = img_len[mate], txt_len[mate]
    flag = jnp.where(flags[c, g] == 1, 1.0, 0.0).astype(F32)

    def source(i, first):
        return text_h.at[chunk(i)] if i == first else txt.at[0, chunk(i)]

    to_right = [
        remote(source(i, 0), txt.at[2, chunk(i)], ts.at[i], tr.at[i], {"mp": right})
        for i in range(4)
    ]
    to_left = [
        remote(source(i, 2), txt.at[1, chunk(i)], ts.at[4 + i], tr.at[4 + i], {"mp": left})
        for i in range(4)
    ]
    on_right = [
        remote(txt.at[2, chunk(i)], txt.at[3, chunk(i)], ts.at[8 + i], tr.at[8 + i], {"mp": right})
        for i in (0, 1)
    ]
    on_left = [
        remote(txt.at[1, chunk(i)], txt.at[3, chunk(i)], ts.at[8 + i], tr.at[8 + i], {"mp": left})
        for i in (2, 3)
    ]

    def norm_text(i, slot=0):
        x = (text[chunk(i), :] if slot == 0 else txt[slot, chunk(i), :]).astype(F32)
        center = x - jnp.mean(x, -1, keepdims=True)
        spread = jnp.mean(center * center, -1, keepdims=True)
        y = center * lax.rsqrt(spread + 1e-06) * (1.0 + mtxt[step, 1:2, :]) + mtxt[step, 0:1, :]
        txt[slot, chunk(i), :] = y.astype(BF16)

    pl.semaphore_wait(barrier, 5)
    to_right[0].start()
    to_left[2].start()

    quarter = half // 2
    e_row = lax.broadcasted_iota(jnp.int32, (ch, 2 * ch), 0)
    e_col = lax.broadcasted_iota(jnp.int32, (ch, 2 * ch), 1)
    twice = jnp.where((e_col == e_row) | (e_col == e_row + ch), 1.0, 0.0).astype(BF16)
    c_lat.wait()
    lines = lax.dot_general(
        lat[:, pl.ds(pl.multiple_of((1 - c) * half, half), half)].astype(BF16), twice,
        (((0,), (0,)), ((), ())), preferred_element_type=F32,
    )
    lane = lax.broadcasted_iota(jnp.int32, (quarter, 2 * ch), 1)
    lall[0, 0] = jnp.where(lane < ch, lines[0:quarter], lines[quarter:]).astype(BF16)
    lat_out = [
        remote(
            lall.at[0, 0], lall.at[0, 4 - k], ls.at[k - 1], lr.at[k - 1],
            {"mp": lax.rem(m + k, n_mp)},
        )
        for k in (1, 2, 3)
    ]
    for copy in lat_out:
        copy.start()

    c_mtxt.wait()
    c_text.wait()
    c_mimg.wait()
    c_wq = [
        local_copy(wq_h.at[:, pl.ds(h * 3 * HD, 3 * HD)], wq.at[h], 5 + h) for h in range(heads)
    ]
    c_wt = local_copy(wt_h, wt, 5 + heads)
    norm_text(1)
    to_right[1].start()
    norm_text(3)
    to_left[3].start()
    norm_text(2)
    to_right[2].start()
    norm_text(0)
    to_left[0].start()
    to_right[3].start()
    to_left[1].start()
    c_wo = local_copy(wo_h, wo, 6 + heads)
    c_wf = local_copy(wf_h, wf, 7 + heads)
    c_mfin = local_copy(mfin_h, mfin, 8 + heads)

    c_win.wait()
    w = win[...].astype(F32)
    w = w - jnp.mean(w, -1, keepdims=True)
    w_high, w_low = split(w)
    wx[0:ch, :] = w_high
    wx[ch : 2 * ch, :] = w_low
    s_high, s_low = split(w * (1.0 + mimg[1, pl.ds(step, 1), :]))
    lhs[0:ch, :] = s_high
    lhs[ch : 2 * ch, :] = s_low
    b_high, b_low = split(mimg[0, pl.ds(step, 1), :])
    b_row = lax.broadcasted_iota(jnp.int32, (16, d), 0)
    lhs[2 * ch :, :] = jnp.where(
        b_row == 0, b_high.astype(F32), jnp.where(b_row == 1, b_low.astype(F32), 0.0)
    ).astype(BF16)

    def fill_mask(ref, img_live, txt_live, on):
        spot = lax.broadcasted_iota(jnp.int32, (half, HD), 0)
        for side in range(2):
            place = (1 - c) if side == 0 else c
            for k in range(4):
                start = lax.rem(m + k, n_mp) * rows + place * half
                at = side * 4 * half + k * half
                ref[at : at + half, :] = jnp.where(spot + start < img_live, on, 0.0).astype(BF16)
        spot_t = lax.broadcasted_iota(jnp.int32, (trows, HD), 0)
        for k in range(4):
            start = lax.rem(m + TEXT_FROM[k], n_mp) * trows
            place = jnp.where((spot_t >= part) & (spot_t < 2 * part), spot_t + part, jnp.where(
                (spot_t >= 2 * part) & (spot_t < 3 * part), spot_t - part, spot_t
            )) if k == 3 else spot_t
            ref[img + k * trows : img + (k + 1) * trows, :] = jnp.where(
                place + start < txt_live, on, 0.0
            ).astype(BF16)

    fill_mask(mask, il, tl, 1.0)
    fill_mask(maskm, il_m, tl_m, flag)

    for h in range(heads):
        c_wq[h].wait()
        full = dot(lhs[...], wq[h])
        fold = full[0:ch] + full[ch : 2 * ch]
        high, low = split(fold)
        rhs[h, 0:ch, :] = high
        rhs[h, ch : 2 * ch, :] = high
        rhs[h, 2 * ch : 3 * ch, :] = low
        rhs[h, 3 * ch : 4 * ch, :] = low
        bias[h] = full[2 * ch : 2 * ch + 8]
    for copy in lat_out:
        copy.wait_recv()
    lat_swap = remote(lall.at[0], lall.at[1], ls.at[3], lr.at[3], {"cfg": 1 - c})
    lat_swap.start()
    q_gain = qg[...] * (HD ** (-0.5) * math.log2(math.e))
    k_gain = kg[...]
    block_rows = 4 * half

    def text_block(lhs_t, first, i):
        n = lhs_t.shape[0]
        span = slice(img + first, img + first + n)
        copies = []
        for h in range(heads):
            x = dot(lhs_t, wt[:, h * 2 * HD : (h + 1) * 2 * HD])
            kv[h, span, 0:HD] = head_norm(x[:, 0:HD], k_gain).astype(BF16)
            kv[h, span, HD : 2 * HD] = x[:, HD:].astype(BF16) * mask[span, :]
            rows_t = pl.ds(img + first, n)
            copy = remote(
                kv.at[h, rows_t], kvm.at[h, rows_t], ks.at[i * heads + h], kr.at[i * heads + h],
                {"group": mate},
            )
            copy.start()
            copies.append(copy)
        return copies

    c_wt.wait()
    kv_txt = text_block(txt[0], 0, 1)
    lat_swap.wait_recv()
    wide = min(d, 512)

    def image_block(side, carry):
        held = jnp.concatenate([lall[side, k] for k in range(4)], axis=0)
        pick = lax.broadcasted_iota(jnp.int32, (2 * ch, 2 * ch), 0)
        lane_of = lax.rem(lax.broadcasted_iota(jnp.int32, (2 * ch, 2 * ch), 1), ch)
        top = dot(held, jnp.where(pick == lane_of, 1.0, 0.0).astype(BF16))
        low = dot(held, jnp.where(pick == lane_of + ch, 1.0, 0.0).astype(BF16))
        pieces = []
        for k in range(4):
            pieces += [top[k * quarter : (k + 1) * quarter], low[k * quarter : (k + 1) * quarter]]
        lat2 = jnp.concatenate(pieces, axis=0)
        lat2b = lat2.astype(BF16)
        squares = jnp.zeros((block_rows, HD), F32)
        for j in range(d // wide):
            x = dot(lat2b, wx[:, j * wide : (j + 1) * wide])
            xc[side, :, j * wide : (j + 1) * wide] = x[0:half]
            for k in range(wide // HD):
                piece = x[:, k * HD : (k + 1) * HD]
                squares = squares + piece * piece
        scaled = lat2 * lax.rsqrt(jnp.sum(squares, -1, keepdims=True) / d + 1e-06)
        scaled_high = scaled.astype(BF16).astype(F32)
        lanes = lax.broadcasted_iota(jnp.int32, (block_rows, 2 * ch), 1)
        block = jnp.where(lanes < ch, scaled_high, scaled - scaled_high).astype(BF16)
        block = jnp.concatenate([block, block], axis=1)
        at = pl.ds(pl.multiple_of(side * block_rows, block_rows), block_rows)
        for h in range(heads):
            x = dot(block, rhs[h]) + (bias[h, 0:1, :] + bias[h, 1:2, :])
            q[h, at, :] = head_norm(x[:, 0:HD], q_gain).astype(BF16)
            kv[h, at, 0:HD] = head_norm(x[:, HD : 2 * HD], k_gain).astype(BF16)
            kv[h, at, HD : 2 * HD] = x[:, 2 * HD :].astype(BF16) * mask[at, :]
        return carry

    lax.fori_loop(0, 2, image_block, 0)
    kv_img = [
        remote(
            kv.at[h, pl.ds(0, img)], kvm.at[h, pl.ds(0, img)], ks.at[h], kr.at[h],
            {"group": mate},
        )
        for h in range(heads)
    ]
    for copy in kv_img:
        copy.start()

    on = flag.astype(BF16)

    def keys(h, parts):
        return jnp.concatenate([ref[h, lo : lo + n, 0:HD] for ref, lo, n in parts], axis=0)

    def values(h, parts):
        rows_v = []
        for ref, lo, n in parts:
            v = ref[h, lo : lo + n, HD : 2 * HD]
            if ref is kvm:
                v = v * on
            live = (maskm if ref is kvm else mask)[lo : lo + n, :]
            rows_v.append(jnp.concatenate([v, live], axis=1))
        return jnp.concatenate(rows_v, axis=0)

    def attend(h, at, parts):
        p = jnp.exp2(nt_dot(q[h, at, :], keys(h, parts))).astype(BF16)
        return dot(p, values(h, parts))

    def each_side(fn):
        def run(side, carry):
            at = pl.ds(pl.multiple_of(side * block_rows, block_rows), block_rows)
            for h in range(heads):
                fn(h, at)
            return carry

        lax.fori_loop(0, 2, run, 0)

    def own_image(h, at):
        acc[h, at, :] = attend(h, at, [(kv, 0, img)])

    each_side(own_image)

    to_right[0].wait_recv()
    norm_text(0, slot=2)
    on_right[0].start()
    to_left[2].wait_recv()
    norm_text(2, slot=1)
    on_left[0].start()
    for copy in kv_img:
        copy.wait_recv()

    def mate_image(h, at):
        acc[h, at, :] += attend(h, at, [(kvm, 0, img)])

    each_side(mate_image)

    to_right[1].wait_recv()
    on_right[1].start()
    to_left[3].wait_recv()
    on_left[1].start()
    to_right[2].wait_recv()
    to_right[3].wait_recv()
    to_left[0].wait_recv()
    to_left[1].wait_recv()
    kv_txt += text_block(jnp.concatenate([txt[1], txt[2]], axis=0), trows, 2)
    for copy in kv_txt:
        copy.wait_recv()

    def most_text(h, at):
        acc[h, at, :] += attend(h, at, [(kv, img, 3 * trows), (kvm, img, 3 * trows)])

    each_side(most_text)

    kv_last = []
    for i in range(2):
        on_right[i].wait_recv()
        on_left[i].wait_recv()
        lhs_t = jnp.concatenate([txt[3, chunk(i), :], txt[3, chunk(2 + i), :]], axis=0)
        kv_last.append(text_block(lhs_t, 3 * trows + 2 * i * part, 3 + i))
    last = img + 3 * trows

    mixes = []
    for side in range(2):
        copies = {k: [] for k in (1, 2, 3)}
        for h in range(heads):
            if side == 0:
                kv_last[0][h].wait_recv()
                kv_last[1][h].wait_recv()
            at = slice(side * block_rows, (side + 1) * block_rows)
            total = acc[h, at, :] + attend(h, at, [(kv, last, trows), (kvm, last, trows)])
            share = (total[:, 0:HD] / total[:, HD : 2 * HD]).astype(BF16)
            for k in range(4):
                mix[side, k, h] = share[k * half : (k + 1) * half]
            for k in (2, 1, 3):
                i = (side * 3 + k - 1) * heads + h
                copy = remote(
                    mix.at[side, k, h], mixr.at[side, 3 - k, h], ms.at[i], mr.at[i],
                    {"mp": lax.rem(m + k, n_mp)},
                )
                copy.start()
                copies[k].append(copy)
        mixes.append(copies)

    def project(side, ref, k, first):
        base = pl.multiple_of(lax.rem(m + k, n_mp) * (heads * HD), heads * HD)
        own = jnp.concatenate([ref[h] for h in range(heads)], axis=1)
        for j in range(d // wide):
            cols = slice(j * wide, (j + 1) * wide)
            x = mimg[2, pl.ds(step, 1), cols] * dot(own, wo[pl.ds(base, heads * HD), cols])
            att[side, :, cols] = (xc if first else att)[side, :, cols] + x

    def finish(side):
        small = min(half, 32)
        for i in range(half // small):
            at = slice(i * small, (i + 1) * small)
            x = att[side, at, :]
            center = x - jnp.mean(x, -1, keepdims=True)
            spread = jnp.mean(center * center, -1, keepdims=True)
            y = center * lax.rsqrt(spread + 1e-06) * (1.0 + mfin[step, 1:2, :]) + mfin[step, 0:1, :]
            fin[at, :] = y.astype(BF16)
        return nt_dot(wf[...], fin[...])

    c_wo.wait()
    project(0, mix.at[0, 0], 0, True)
    project(1, mix.at[1, 0], 0, True)
    c_wf.wait()
    c_mfin.wait()
    for k in (1, 3, 2):
        for copy in mixes[0][k]:
            copy.wait_recv()
        project(0, mixr.at[0, 3 - k], 4 - k, False)
    vsend[...] = finish(0)
    swap = remote(vsend, vrecv, vs.at[0], vr.at[0], {"cfg": 1 - c})
    swap.start()
    for k in (1, 3, 2):
        for copy in mixes[1][k]:
            copy.wait_recv()
        project(1, mixr.at[1, 3 - k], 4 - k, False)
    own = finish(1)
    swap.wait_recv()
    other = vrecv[...]
    cond = jnp.where(c == 0, own, other)
    uncond = jnp.where(c == 0, other, own)
    guided = uncond + guide[g] * (cond - uncond)
    spot = lax.broadcasted_iota(jnp.int32, (ch, half), 1) + (m * rows + c * half)
    guided = jnp.where(spot < il, guided, 0.0)
    out[0] = guided
    out[1] = lat[:, pl.ds(pl.multiple_of(c * half, half), half)] - step_size[step] * guided

    for copy in to_right + to_left + on_right + on_left + lat_out + kv_img + kv_txt + kv_last[0] + kv_last[1]:
        copy.wait_send()
    for copies in mixes:
        for k in (2, 1, 3):
            for copy in copies[k]:
                copy.wait_send()
    swap.wait_send()
    lat_swap.wait_send()


def unpack(both, velocity, moved):
    velocity[...] = both[0]
    moved[...] = both[1]


def local(
    latents, text_hidden, w_img_in, w_img_qkv, w_txt_kv, q_gain, k_gain, w_out, w_final,
    mod_img, mod_txt, mod_final, guide, step_size, img_len, txt_len, split_flag, tstep,
):
    text = text_hidden[0]
    rows, ch = latents.shape
    trows, d = text.shape
    heads = w_img_qkv.shape[1] // (3 * HD)
    img, ntxt = 4 * rows, 4 * trows
    half = rows // 2
    hbm = pl.BlockSpec(memory_space=pl.ANY)
    vmem = pl.BlockSpec(memory_space=pltpu.VMEM)
    smem = pl.BlockSpec(memory_space=pltpu.SMEM)
    dma = pltpu.SemaphoreType.DMA
    out = jax.ShapeDtypeStruct((2, ch, half), F32)
    single = jax.ShapeDtypeStruct((ch, half), F32)
    scratch = [
        pltpu.VMEM((ch, rows), F32),
        pltpu.VMEM(text.shape, BF16),
        pltpu.VMEM(w_img_in.shape, BF16),
        pltpu.VMEM((heads, d, 3 * HD), BF16),
        pltpu.VMEM(w_txt_kv.shape, BF16),
        pltpu.VMEM(w_out.shape, BF16),
        pltpu.VMEM((ch, d), BF16),
        pltpu.VMEM((3, mod_img.shape[0], d), F32),
        pltpu.VMEM(mod_txt.shape, F32),
        pltpu.VMEM(mod_final.shape, F32),
        pltpu.VMEM((4, trows, d), BF16),
        pltpu.VMEM((2, 4, half // 2, 2 * ch), BF16),
        pltpu.VMEM((2 * ch, d), BF16),
        pltpu.VMEM((2 * ch + 16, d), BF16),
        pltpu.VMEM((heads, 4 * ch, 3 * HD), BF16),
        pltpu.VMEM((heads, 8, 3 * HD), F32),
        pltpu.VMEM((2, half, d), F32),
        pltpu.VMEM((heads, img, HD), BF16),
        pltpu.VMEM((heads, img + ntxt, 2 * HD), BF16),
        pltpu.VMEM((heads, img + ntxt, 2 * HD), BF16),
        pltpu.VMEM((img + ntxt, HD), BF16),
        pltpu.VMEM((img + ntxt, HD), BF16),
        pltpu.VMEM((heads, img, 2 * HD), F32),
        pltpu.VMEM((2, half, d), F32),
        pltpu.VMEM((2, 4, heads, half, HD), BF16),
        pltpu.VMEM((2, 3, heads, half, HD), BF16),
        pltpu.VMEM((half, d), BF16),
        pltpu.VMEM((ch, half), F32),
        pltpu.VMEM((ch, half), F32),
        dma((13 + heads,)),
        dma((12,)), dma((12,)),
        dma((4,)), dma((4,)),
        dma((5 * heads,)), dma((5 * heads,)),
        dma((6 * heads,)), dma((6 * heads,)),
        dma((1,)), dma((1,)),
    ]
    both = pl.pallas_call(
        body,
        out_shape=out,
        in_specs=[hbm] * 10 + [vmem] * 2 + [smem] * 6,
        out_specs=vmem,
        scratch_shapes=scratch,
        compiler_params=pltpu.CompilerParams(
            collective_id=0, has_side_effects=True, vmem_limit_bytes=61 * 1024 * 1024
        ),
        name="guided_step",
    )(
        latents.T, text, w_img_in, w_img_qkv, w_txt_kv, w_out, w_final.T,
        jnp.transpose(mod_img, (1, 0, 2)), mod_txt, mod_final,
        q_gain[None], k_gain[None], guide, step_size, img_len, txt_len, split_flag, tstep,
    )
    velocity, moved = pl.pallas_call(
        unpack,
        out_shape=(single, single),
        in_specs=[vmem],
        out_specs=(vmem, vmem),
        name="unpack",
    )(both)
    return velocity.T[None], moved.T[None]


def solution(mesh):
    rep = P()
    placed = (
        P(("group", "mp"), None), P("cfg", ("group", "mp"), None), rep,
        P(None, "mp"), P(None, "mp"),
    ) + (rep,) * 13
    out = P("cfg", ("group", "mp"), None)
    return jax.shard_map(
        local, mesh=mesh, in_specs=placed, out_specs=(out, out), check_vma=False
    )
```

```python
import functools
import math

import jax
import jax.numpy as jnp
from jax import lax
from jax.experimental import pallas as pl
from jax.experimental.pallas import tpu as pltpu
from jax.sharding import PartitionSpec as P

HD = 128
F32 = jnp.float32
BF16 = jnp.bfloat16
MESH = pl.DeviceIdType.MESH
TEXT_FROM = (0, 1, 3, 2)


def nt_dot(a, b):
    return lax.dot_general(a, b, (((1,), (1,)), ((), ())), preferred_element_type=F32)


def dot(a, b):
    return jnp.dot(a, b, preferred_element_type=F32)


def head_norm(values, gain):
    return values * lax.rsqrt(jnp.mean(values * values, -1, keepdims=True) + 1e-06) * gain


def split(values):
    high = values.astype(BF16)
    return high, (values - high.astype(F32)).astype(BF16)


def body(
    lat_h, text_h, win_h, wq_h, wt_h, wo_h, wf_h, mimg_h, mtxt_h, mfin_h,
    qg, kg, guide, step_size, img_len, txt_len, flags, tstep,
    out,
    lat, text, win, wq, wt, wo, wf, mimg, mtxt, mfin,
    txt, lall, wx, lhs, rhs, bias, xc, q, kv, kvm, mask, maskm, acc, att,
    mix, mixr, fin, vsend, vrecv,
    lsem, ts, tr, ls, lr, ks, kr, ms, mr, vs, vr,
):
    c = lax.axis_index("cfg")
    g = lax.axis_index("group")
    m = lax.axis_index("mp")
    n_mp = 4
    right, left = lax.rem(m + 1, n_mp), lax.rem(m + 3, n_mp)
    mate = g + 1 - 2 * lax.rem(g, 2)
    ch, rows = lat_h.shape
    trows, d = text_h.shape
    heads = wq_h.shape[1] // (3 * HD)
    img, ntxt = rows * n_mp, trows * n_mp
    half = rows // 2
    part = trows // 4

    def chunk(i):
        return pl.ds(i * part, part)

    def local_copy(src, dst, i):
        copy = pltpu.make_async_copy(src, dst, lsem.at[i])
        copy.start()
        return copy

    c_lat = local_copy(lat_h, lat, 2)
    c_win = local_copy(win_h, win, 3)
    c_mtxt = local_copy(mtxt_h, mtxt, 1)
    c_text = local_copy(text_h, text, 0)
    c_mimg = local_copy(mimg_h, mimg, 4)
    c_wq = [
        local_copy(wq_h.at[:, pl.ds(h * 3 * HD, 3 * HD)], wq.at[h], 5 + h) for h in range(heads)
    ]
    c_wt = local_copy(wt_h, wt, 5 + heads)

    barrier = pltpu.get_barrier_semaphore()
    for k in (1, 2, 3):
        pl.semaphore_signal(
            barrier, inc=1, device_id={"mp": lax.rem(m + k, n_mp)}, device_id_type=MESH
        )
    pl.semaphore_signal(barrier, inc=1, device_id={"group": mate}, device_id_type=MESH)
    pl.semaphore_signal(barrier, inc=1, device_id={"cfg": 1 - c}, device_id_type=MESH)

    def remote(src, dst, ssem, rsem, device):
        return pltpu.make_async_remote_copy(
            src_ref=src, dst_ref=dst, send_sem=ssem, recv_sem=rsem,
            device_id=device, device_id_type=MESH,
        )

    step = tstep[g]
    il, tl = img_len[g], txt_len[g]
    il_m, tl_m = img_len[mate], txt_len[mate]
    flag = jnp.where(flags[c, g] == 1, 1.0, 0.0).astype(F32)

    def source(i, first):
        return text_h.at[chunk(i)] if i == first else txt.at[0, chunk(i)]

    to_right = [
        remote(source(i, 0), txt.at[2, chunk(i)], ts.at[i], tr.at[i], {"mp": right})
        for i in range(4)
    ]
    to_left = [
        remote(source(i, 2), txt.at[1, chunk(i)], ts.at[4 + i], tr.at[4 + i], {"mp": left})
        for i in range(4)
    ]
    on_right = [
        remote(txt.at[2, chunk(i)], txt.at[3, chunk(i)], ts.at[8 + i], tr.at[8 + i], {"mp": right})
        for i in (0, 1)
    ]
    on_left = [
        remote(txt.at[1, chunk(i)], txt.at[3, chunk(i)], ts.at[8 + i], tr.at[8 + i], {"mp": left})
        for i in (2, 3)
    ]

    def norm_text(i, slot=0):
        x = (text[chunk(i), :] if slot == 0 else txt[slot, chunk(i), :]).astype(F32)
        center = x - jnp.mean(x, -1, keepdims=True)
        spread = jnp.mean(center * center, -1, keepdims=True)
        y = center * lax.rsqrt(spread + 1e-06) * (1.0 + mtxt[step, 1:2, :]) + mtxt[step, 0:1, :]
        txt[slot, chunk(i), :] = y.astype(BF16)

    pl.semaphore_wait(barrier, 5)
    to_right[0].start()
    to_left[2].start()

    quarter = half // 2
    e_row = lax.broadcasted_iota(jnp.int32, (ch, 2 * ch), 0)
    e_col = lax.broadcasted_iota(jnp.int32, (ch, 2 * ch), 1)
    twice = jnp.where((e_col == e_row) | (e_col == e_row + ch), 1.0, 0.0).astype(BF16)
    c_lat.wait()
    lines = lax.dot_general(
        lat[:, pl.ds(pl.multiple_of((1 - c) * half, half), half)].astype(BF16), twice,
        (((0,), (0,)), ((), ())), preferred_element_type=F32,
    )
    lane = lax.broadcasted_iota(jnp.int32, (quarter, 2 * ch), 1)
    lall[0, 0] = jnp.where(lane < ch, lines[0:quarter], lines[quarter:]).astype(BF16)
    lat_out = [
        remote(
            lall.at[0, 0], lall.at[0, 4 - k], ls.at[k - 1], lr.at[k - 1],
            {"mp": lax.rem(m + k, n_mp)},
        )
        for k in (1, 2, 3)
    ]
    for copy in lat_out:
        copy.start()

    c_mtxt.wait()
    c_text.wait()
    c_mimg.wait()
    norm_text(1)
    to_right[1].start()
    norm_text(3)
    to_left[3].start()
    norm_text(2)
    to_right[2].start()
    norm_text(0)
    to_left[0].start()
    to_right[3].start()
    to_left[1].start()

    c_win.wait()
    w = win[...].astype(F32)
    w = w - jnp.mean(w, -1, keepdims=True)
    w_high, w_low = split(w)
    wx[0:ch, :] = w_high
    wx[ch : 2 * ch, :] = w_low
    s_high, s_low = split(w * (1.0 + mimg[1, pl.ds(step, 1), :]))
    lhs[0:ch, :] = s_high
    lhs[ch : 2 * ch, :] = s_low
    b_high, b_low = split(mimg[0, pl.ds(step, 1), :])
    b_row = lax.broadcasted_iota(jnp.int32, (16, d), 0)
    lhs[2 * ch :, :] = jnp.where(
        b_row == 0, b_high.astype(F32), jnp.where(b_row == 1, b_low.astype(F32), 0.0)
    ).astype(BF16)

    def fill_mask(ref, img_live, txt_live, on):
        spot = lax.broadcasted_iota(jnp.int32, (half, HD), 0)
        for side in range(2):
            place = (1 - c) if side == 0 else c
            for k in range(4):
                start = lax.rem(m + k, n_mp) * rows + place * half
                at = side * 4 * half + k * half
                ref[at : at + half, :] = jnp.where(spot + start < img_live, on, 0.0).astype(BF16)
        spot_t = lax.broadcasted_iota(jnp.int32, (trows, HD), 0)
        for k in range(4):
            start = lax.rem(m + TEXT_FROM[k], n_mp) * trows
            ref[img + k * trows : img + (k + 1) * trows, :] = jnp.where(
                spot_t + start < txt_live, on, 0.0
            ).astype(BF16)

    fill_mask(mask, il, tl, 1.0)
    fill_mask(maskm, il_m, tl_m, flag)

    for h in range(heads):
        c_wq[h].wait()
        full = dot(lhs[...], wq[h])
        fold = full[0:ch] + full[ch : 2 * ch]
        high, low = split(fold)
        rhs[h, 0:ch, :] = high
        rhs[h, ch : 2 * ch, :] = high
        rhs[h, 2 * ch : 3 * ch, :] = low
        rhs[h, 3 * ch : 4 * ch, :] = low
        bias[h] = full[2 * ch : 2 * ch + 8]
    for copy in lat_out:
        copy.wait_recv()
    lat_swap = remote(lall.at[0], lall.at[1], ls.at[3], lr.at[3], {"cfg": 1 - c})
    lat_swap.start()
    q_gain = qg[...] * (HD ** (-0.5) * math.log2(math.e))
    k_gain = kg[...]
    block_rows = 4 * half

    def text_block(lhs_t, first, i):
        n = lhs_t.shape[0]
        span = slice(img + first, img + first + n)
        copies = []
        for h in range(heads):
            x = dot(lhs_t, wt[:, h * 2 * HD : (h + 1) * 2 * HD])
            kv[h, span, 0:HD] = head_norm(x[:, 0:HD], k_gain).astype(BF16)
            kv[h, span, HD : 2 * HD] = x[:, HD:].astype(BF16) * mask[span, :]
            rows_t = pl.ds(img + first, n)
            copy = remote(
                kv.at[h, rows_t], kvm.at[h, rows_t], ks.at[i * heads + h], kr.at[i * heads + h],
                {"group": mate},
            )
            copy.start()
            copies.append(copy)
        return copies

    c_wt.wait()
    c_wo = local_copy(wo_h, wo, 6 + heads)
    c_wf = local_copy(wf_h, wf, 7 + heads)
    c_mfin = local_copy(mfin_h, mfin, 8 + heads)
    kv_txt = text_block(txt[0], 0, 1)
    to_right[0].wait_recv()
    norm_text(0, slot=2)
    on_right[0].start()
    to_left[2].wait_recv()
    norm_text(2, slot=1)
    on_left[0].start()
    lat_swap.wait_recv()
    wide = min(d, 512)

    def image_block(side, carry):
        held = jnp.concatenate([lall[side, k] for k in range(4)], axis=0)
        pick = lax.broadcasted_iota(jnp.int32, (2 * ch, 2 * ch), 0)
        lane_of = lax.rem(lax.broadcasted_iota(jnp.int32, (2 * ch, 2 * ch), 1), ch)
        top = dot(held, jnp.where(pick == lane_of, 1.0, 0.0).astype(BF16))
        low = dot(held, jnp.where(pick == lane_of + ch, 1.0, 0.0).astype(BF16))
        pieces = []
        for k in range(4):
            pieces += [top[k * quarter : (k + 1) * quarter], low[k * quarter : (k + 1) * quarter]]
        lat2 = jnp.concatenate(pieces, axis=0)
        lat2b = lat2.astype(BF16)
        squares = jnp.zeros((block_rows, HD), F32)
        for j in range(d // wide):
            x = dot(lat2b, wx[:, j * wide : (j + 1) * wide])
            xc[side, :, j * wide : (j + 1) * wide] = x[0:half]
            for k in range(wide // HD):
                piece = x[:, k * HD : (k + 1) * HD]
                squares = squares + piece * piece
        scaled = lat2 * lax.rsqrt(jnp.sum(squares, -1, keepdims=True) / d + 1e-06)
        scaled_high = scaled.astype(BF16).astype(F32)
        lanes = lax.broadcasted_iota(jnp.int32, (block_rows, 2 * ch), 1)
        block = jnp.where(lanes < ch, scaled_high, scaled - scaled_high).astype(BF16)
        block = jnp.concatenate([block, block], axis=1)
        at = pl.ds(pl.multiple_of(side * block_rows, block_rows), block_rows)
        for h in range(heads):
            x = dot(block, rhs[h]) + (bias[h, 0:1, :] + bias[h, 1:2, :])
            q[h, at, :] = head_norm(x[:, 0:HD], q_gain).astype(BF16)
            kv[h, at, 0:HD] = head_norm(x[:, HD : 2 * HD], k_gain).astype(BF16)
            kv[h, at, HD : 2 * HD] = x[:, 2 * HD :].astype(BF16) * mask[at, :]
        return carry

    lax.fori_loop(0, 2, image_block, 0)
    kv_img = [
        remote(
            kv.at[h, pl.ds(0, img)], kvm.at[h, pl.ds(0, img)], ks.at[h], kr.at[h],
            {"group": mate},
        )
        for h in range(heads)
    ]
    for copy in kv_img:
        copy.start()

    on = flag.astype(BF16)

    def keys(h, parts):
        return jnp.concatenate([ref[h, lo : lo + n, 0:HD] for ref, lo, n in parts], axis=0)

    def values(h, parts):
        rows_v = []
        for ref, lo, n in parts:
            v = ref[h, lo : lo + n, HD : 2 * HD]
            if ref is kvm:
                v = v * on
            live = (maskm if ref is kvm else mask)[lo : lo + n, :]
            rows_v.append(jnp.concatenate([v, live], axis=1))
        return jnp.concatenate(rows_v, axis=0)

    def attend(h, at, parts):
        p = jnp.exp2(nt_dot(q[h, at, :], keys(h, parts))).astype(BF16)
        return dot(p, values(h, parts))

    def each_side(fn):
        def run(side, carry):
            at = pl.ds(pl.multiple_of(side * block_rows, block_rows), block_rows)
            for h in range(heads):
                fn(h, at)
            return carry

        lax.fori_loop(0, 2, run, 0)

    def own_image(h, at):
        acc[h, at, :] = attend(h, at, [(kv, 0, img)])

    each_side(own_image)

    for copy in kv_img:
        copy.wait_recv()

    def mate_image(h, at):
        acc[h, at, :] += attend(h, at, [(kvm, 0, img)])

    each_side(mate_image)

    to_right[1].wait_recv()
    on_right[1].start()
    to_left[3].wait_recv()
    on_left[1].start()
    to_right[2].wait_recv()
    to_right[3].wait_recv()
    to_left[0].wait_recv()
    to_left[1].wait_recv()
    kv_txt += text_block(jnp.concatenate([txt[1], txt[2]], axis=0), trows, 2)
    for copy in kv_txt:
        copy.wait_recv()

    def most_text(h, at):
        acc[h, at, :] += attend(h, at, [(kv, img, 3 * trows), (kvm, img, 3 * trows)])

    each_side(most_text)

    for copy in on_right + on_left:
        copy.wait_recv()
    kv_last = text_block(txt[3], 3 * trows, 3)
    last = img + 3 * trows

    mixes = []
    for side in range(2):
        copies = {k: [] for k in (1, 2, 3)}
        for h in range(heads):
            if side == 0:
                kv_last[h].wait_recv()
            at = slice(side * block_rows, (side + 1) * block_rows)
            total = acc[h, at, :] + attend(h, at, [(kv, last, trows), (kvm, last, trows)])
            share = (total[:, 0:HD] / total[:, HD : 2 * HD]).astype(BF16)
            for k in range(4):
                mix[side, k, h] = share[k * half : (k + 1) * half]
            for k in (2, 1, 3):
                i = (side * 3 + k - 1) * heads + h
                copy = remote(
                    mix.at[side, k, h], mixr.at[side, 3 - k, h], ms.at[i], mr.at[i],
                    {"mp": lax.rem(m + k, n_mp)},
                )
                copy.start()
                copies[k].append(copy)
        mixes.append(copies)

    def project(side, ref, k, first):
        base = pl.multiple_of(lax.rem(m + k, n_mp) * (heads * HD), heads * HD)
        own = jnp.concatenate([ref[h] for h in range(heads)], axis=1)
        for j in range(d // wide):
            cols = slice(j * wide, (j + 1) * wide)
            x = dot(own, wo[pl.ds(base, heads * HD), cols])
            att[side, :, cols] = x if first else att[side, :, cols] + x

    def finish(side):
        small = min(half, 32)
        for i in range(half // small):
            at = slice(i * small, (i + 1) * small)
            x = xc[side, at, :] + mimg[2, pl.ds(step, 1), :] * att[side, at, :]
            center = x - jnp.mean(x, -1, keepdims=True)
            spread = jnp.mean(center * center, -1, keepdims=True)
            y = center * lax.rsqrt(spread + 1e-06) * (1.0 + mfin[step, 1:2, :]) + mfin[step, 0:1, :]
            fin[at, :] = y.astype(BF16)
        return nt_dot(wf[...], fin[...])

    c_wo.wait()
    project(0, mix.at[0, 0], 0, True)
    project(1, mix.at[1, 0], 0, True)
    c_wf.wait()
    c_mfin.wait()
    for k in (2, 1, 3):
        for copy in mixes[0][k]:
            copy.wait_recv()
        project(0, mixr.at[0, 3 - k], 4 - k, False)
    vsend[...] = finish(0)
    swap = remote(vsend, vrecv, vs.at[0], vr.at[0], {"cfg": 1 - c})
    swap.start()
    for k in (2, 1, 3):
        for copy in mixes[1][k]:
            copy.wait_recv()
        project(1, mixr.at[1, 3 - k], 4 - k, False)
    own = finish(1)
    swap.wait_recv()
    other = vrecv[...]
    cond = jnp.where(c == 0, own, other)
    uncond = jnp.where(c == 0, other, own)
    guided = uncond + guide[g] * (cond - uncond)
    spot = lax.broadcasted_iota(jnp.int32, (ch, half), 1) + (m * rows + c * half)
    guided = jnp.where(spot < il, guided, 0.0)
    out[0] = guided
    out[1] = lat[:, pl.ds(pl.multiple_of(c * half, half), half)] - step_size[step] * guided

    for copy in to_right + to_left + on_right + on_left + lat_out + kv_img + kv_txt + kv_last:
        copy.wait_send()
    for copies in mixes:
        for k in (2, 1, 3):
            for copy in copies[k]:
                copy.wait_send()
    swap.wait_send()
    lat_swap.wait_send()


def unpack(both, velocity, moved):
    velocity[...] = both[0]
    moved[...] = both[1]


def local(
    latents, text_hidden, w_img_in, w_img_qkv, w_txt_kv, q_gain, k_gain, w_out, w_final,
    mod_img, mod_txt, mod_final, guide, step_size, img_len, txt_len, split_flag, tstep,
):
    text = text_hidden[0]
    rows, ch = latents.shape
    trows, d = text.shape
    heads = w_img_qkv.shape[1] // (3 * HD)
    img, ntxt = 4 * rows, 4 * trows
    half = rows // 2
    hbm = pl.BlockSpec(memory_space=pl.ANY)
    vmem = pl.BlockSpec(memory_space=pltpu.VMEM)
    smem = pl.BlockSpec(memory_space=pltpu.SMEM)
    dma = pltpu.SemaphoreType.DMA
    out = jax.ShapeDtypeStruct((2, ch, half), F32)
    single = jax.ShapeDtypeStruct((ch, half), F32)
    scratch = [
        pltpu.VMEM((ch, rows), F32),
        pltpu.VMEM(text.shape, BF16),
        pltpu.VMEM(w_img_in.shape, BF16),
        pltpu.VMEM((heads, d, 3 * HD), BF16),
        pltpu.VMEM(w_txt_kv.shape, BF16),
        pltpu.VMEM(w_out.shape, BF16),
        pltpu.VMEM((ch, d), BF16),
        pltpu.VMEM((3, mod_img.shape[0], d), F32),
        pltpu.VMEM(mod_txt.shape, F32),
        pltpu.VMEM(mod_final.shape, F32),
        pltpu.VMEM((4, trows, d), BF16),
        pltpu.VMEM((2, 4, half // 2, 2 * ch), BF16),
        pltpu.VMEM((2 * ch, d), BF16),
        pltpu.VMEM((2 * ch + 16, d), BF16),
        pltpu.VMEM((heads, 4 * ch, 3 * HD), BF16),
        pltpu.VMEM((heads, 8, 3 * HD), F32),
        pltpu.VMEM((2, half, d), F32),
        pltpu.VMEM((heads, img, HD), BF16),
        pltpu.VMEM((heads, img + ntxt, 2 * HD), BF16),
        pltpu.VMEM((heads, img + ntxt, 2 * HD), BF16),
        pltpu.VMEM((img + ntxt, HD), BF16),
        pltpu.VMEM((img + ntxt, HD), BF16),
        pltpu.VMEM((heads, img, 2 * HD), F32),
        pltpu.VMEM((2, half, d), F32),
        pltpu.VMEM((2, 4, heads, half, HD), BF16),
        pltpu.VMEM((2, 3, heads, half, HD), BF16),
        pltpu.VMEM((half, d), BF16),
        pltpu.VMEM((ch, half), F32),
        pltpu.VMEM((ch, half), F32),
        dma((13 + heads,)),
        dma((12,)), dma((12,)),
        dma((4,)), dma((4,)),
        dma((4 * heads,)), dma((4 * heads,)),
        dma((6 * heads,)), dma((6 * heads,)),
        dma((1,)), dma((1,)),
    ]
    both = pl.pallas_call(
        body,
        out_shape=out,
        in_specs=[hbm] * 10 + [vmem] * 2 + [smem] * 6,
        out_specs=vmem,
        scratch_shapes=scratch,
        compiler_params=pltpu.CompilerParams(
            collective_id=0, has_side_effects=True, vmem_limit_bytes=61 * 1024 * 1024
        ),
        name="guided_step",
    )(
        latents.T, text, w_img_in, w_img_qkv, w_txt_kv, w_out, w_final.T,
        jnp.transpose(mod_img, (1, 0, 2)), mod_txt, mod_final,
        q_gain[None], k_gain[None], guide, step_size, img_len, txt_len, split_flag, tstep,
    )
    velocity, moved = pl.pallas_call(
        unpack,
        out_shape=(single, single),
        in_specs=[vmem],
        out_specs=(vmem, vmem),
        name="unpack",
    )(both)
    return velocity.T[None], moved.T[None]


def solution(mesh):
    rep = P()
    placed = (
        P(("group", "mp"), None), P("cfg", ("group", "mp"), None), rep,
        P(None, "mp"), P(None, "mp"),
    ) + (rep,) * 13
    out = P("cfg", ("group", "mp"), None)
    return jax.shard_map(
        local, mesh=mesh, in_specs=placed, out_specs=(out, out), check_vma=False
    )
```

```python
import functools
import math

import jax
import jax.numpy as jnp
from jax import lax
from jax.experimental import pallas as pl
from jax.experimental.pallas import tpu as pltpu
from jax.sharding import PartitionSpec as P

HD = 128
F32 = jnp.float32
BF16 = jnp.bfloat16
MESH = pl.DeviceIdType.MESH
TEXT_FROM = (0, 1, 3, 2)


def nt_dot(a, b):
    return lax.dot_general(a, b, (((1,), (1,)), ((), ())), preferred_element_type=F32)


def dot(a, b):
    return jnp.dot(a, b, preferred_element_type=F32)


def head_norm(values, gain):
    return values * lax.rsqrt(jnp.mean(values * values, -1, keepdims=True) + 1e-06) * gain


def split(values):
    high = values.astype(BF16)
    return high, (values - high.astype(F32)).astype(BF16)


def body(
    lat_h, text_h, win_h, wq_h, wt_h, wo_h, wf_h, mimg_h, mtxt_h, mfin_h,
    qg, kg, guide, step_size, img_len, txt_len, flags, tstep,
    out,
    lat, text, win, wq, wt, wo, wf, mimg, mtxt, mfin,
    txt, lall, wx, lhs, rhs, bias, xc, q, kv, kvm, mask, maskm, acc, att,
    mix, mixr, fin, vsend, vrecv,
    lsem, ts, tr, ls, lr, ks, kr, ms, mr, vs, vr,
):
    c = lax.axis_index("cfg")
    g = lax.axis_index("group")
    m = lax.axis_index("mp")
    n_mp = 4
    right, left = lax.rem(m + 1, n_mp), lax.rem(m + 3, n_mp)
    mate = g + 1 - 2 * lax.rem(g, 2)
    ch, rows = lat_h.shape
    trows, d = text_h.shape
    heads = wq_h.shape[1] // (3 * HD)
    img, ntxt = rows * n_mp, trows * n_mp
    half = rows // 2
    part = trows // 4

    def chunk(i):
        return pl.ds(i * part, part)

    def local_copy(src, dst, i):
        copy = pltpu.make_async_copy(src, dst, lsem.at[i])
        copy.start()
        return copy

    c_lat = local_copy(lat_h, lat, 2)
    c_win = local_copy(win_h, win, 3)
    c_mtxt = local_copy(mtxt_h, mtxt, 1)
    c_text = local_copy(text_h, text, 0)
    c_mimg = local_copy(mimg_h, mimg, 4)

    barrier = pltpu.get_barrier_semaphore()
    for k in (1, 2, 3):
        pl.semaphore_signal(
            barrier, inc=1, device_id={"mp": lax.rem(m + k, n_mp)}, device_id_type=MESH
        )
    pl.semaphore_signal(barrier, inc=1, device_id={"group": mate}, device_id_type=MESH)
    pl.semaphore_signal(barrier, inc=1, device_id={"cfg": 1 - c}, device_id_type=MESH)

    def remote(src, dst, ssem, rsem, device):
        return pltpu.make_async_remote_copy(
            src_ref=src, dst_ref=dst, send_sem=ssem, recv_sem=rsem,
            device_id=device, device_id_type=MESH,
        )

    step = tstep[g]
    il, tl = img_len[g], txt_len[g]
    il_m, tl_m = img_len[mate], txt_len[mate]
    flag = jnp.where(flags[c, g] == 1, 1.0, 0.0).astype(F32)

    def source(i, first):
        return text_h.at[chunk(i)] if i == first else txt.at[0, chunk(i)]

    to_right = [
        remote(source(i, 0), txt.at[2, chunk(i)], ts.at[i], tr.at[i], {"mp": right})
        for i in range(4)
    ]
    to_left = [
        remote(source(i, 2), txt.at[1, chunk(i)], ts.at[4 + i], tr.at[4 + i], {"mp": left})
        for i in range(4)
    ]
    on_right = [
        remote(txt.at[2, chunk(i)], txt.at[3, chunk(i)], ts.at[8 + i], tr.at[8 + i], {"mp": right})
        for i in (0, 1)
    ]
    on_left = [
        remote(txt.at[1, chunk(i)], txt.at[3, chunk(i)], ts.at[8 + i], tr.at[8 + i], {"mp": left})
        for i in (2, 3)
    ]

    def norm_text(i, slot=0):
        x = (text[chunk(i), :] if slot == 0 else txt[slot, chunk(i), :]).astype(F32)
        center = x - jnp.mean(x, -1, keepdims=True)
        spread = jnp.mean(center * center, -1, keepdims=True)
        y = center * lax.rsqrt(spread + 1e-06) * (1.0 + mtxt[step, 1:2, :]) + mtxt[step, 0:1, :]
        txt[slot, chunk(i), :] = y.astype(BF16)

    pl.semaphore_wait(barrier, 5)
    to_right[0].start()
    to_left[2].start()
    c_lat.wait()
    c_win.wait()

    e_row = lax.broadcasted_iota(jnp.int32, (ch, 2 * ch), 0)
    e_col = lax.broadcasted_iota(jnp.int32, (ch, 2 * ch), 1)
    twice = jnp.where((e_col == e_row) | (e_col == e_row + ch), 1.0, 0.0).astype(BF16)
    lat2 = lax.dot_general(
        lat[...].astype(BF16), twice, (((0,), (0,)), ((), ())), preferred_element_type=F32
    )
    w = win[...].astype(F32)
    w = w - jnp.mean(w, -1, keepdims=True)
    w_high, w_low = split(w)
    wx[0:ch, :] = w_high
    wx[ch : 2 * ch, :] = w_low
    lat2b = lat2.astype(BF16)
    squares = jnp.zeros((rows, HD), F32)
    wide = min(d, 512)
    for j in range(d // wide):
        x = dot(lat2b, wx[:, j * wide : (j + 1) * wide])
        xc[1 - c, :, j * wide : (j + 1) * wide] = x[0:half]
        xc[c, :, j * wide : (j + 1) * wide] = x[half:]
        for k in range(wide // HD):
            piece = x[:, k * HD : (k + 1) * HD]
            squares = squares + piece * piece
    rstd = lax.rsqrt(jnp.sum(squares, -1, keepdims=True) / d + 1e-06)
    scaled = lat2 * rstd
    scaled_high = scaled.astype(BF16).astype(F32)
    lane = lax.broadcasted_iota(jnp.int32, (rows, 2 * ch), 1)
    scaled = jnp.where(lane < ch, scaled_high, scaled - scaled_high).astype(BF16)
    lall[1 - c, 0] = scaled[0:half]
    lall[c, 0] = scaled[half:]
    lat_out = [
        remote(
            lall.at[:, 0], lall.at[:, 4 - k], ls.at[k - 1], lr.at[k - 1],
            {"mp": lax.rem(m + k, n_mp)},
        )
        for k in (1, 2, 3)
    ]
    for copy in lat_out:
        copy.start()

    c_mtxt.wait()
    c_text.wait()
    c_mimg.wait()
    c_wq = [
        local_copy(wq_h.at[:, pl.ds(h * 3 * HD, 3 * HD)], wq.at[h], 5 + h) for h in range(heads)
    ]
    c_wt = local_copy(wt_h, wt, 5 + heads)
    norm_text(1)
    to_right[1].start()
    norm_text(3)
    to_left[3].start()
    norm_text(2)
    to_right[2].start()
    norm_text(0)
    to_left[0].start()
    to_right[3].start()
    to_left[1].start()
    c_wo = local_copy(wo_h, wo, 6 + heads)
    c_wf = local_copy(wf_h, wf, 7 + heads)
    c_mfin = local_copy(mfin_h, mfin, 8 + heads)

    s_high, s_low = split(w * (1.0 + mimg[1, pl.ds(step, 1), :]))
    lhs[0:ch, :] = s_high
    lhs[ch : 2 * ch, :] = s_low
    b_high, b_low = split(mimg[0, pl.ds(step, 1), :])
    b_row = lax.broadcasted_iota(jnp.int32, (16, d), 0)
    lhs[2 * ch :, :] = jnp.where(
        b_row == 0, b_high.astype(F32), jnp.where(b_row == 1, b_low.astype(F32), 0.0)
    ).astype(BF16)

    def fill_mask(ref, img_live, txt_live, on):
        spot = lax.broadcasted_iota(jnp.int32, (half, HD), 0)
        for side in range(2):
            place = (1 - c) if side == 0 else c
            for k in range(4):
                start = lax.rem(m + k, n_mp) * rows + place * half
                at = side * 4 * half + k * half
                ref[at : at + half, :] = jnp.where(spot + start < img_live, on, 0.0).astype(BF16)
        spot_t = lax.broadcasted_iota(jnp.int32, (trows, HD), 0)
        for k in range(4):
            start = lax.rem(m + TEXT_FROM[k], n_mp) * trows
            ref[img + k * trows : img + (k + 1) * trows, :] = jnp.where(
                spot_t + start < txt_live, on, 0.0
            ).astype(BF16)

    fill_mask(mask, il, tl, 1.0)
    fill_mask(maskm, il_m, tl_m, flag)

    for h in range(heads):
        c_wq[h].wait()
        full = dot(lhs[...], wq[h])
        fold = full[0:ch] + full[ch : 2 * ch]
        high, low = split(fold)
        rhs[h, 0:ch, :] = high
        rhs[h, ch : 2 * ch, :] = high
        rhs[h, 2 * ch : 3 * ch, :] = low
        rhs[h, 3 * ch : 4 * ch, :] = low
        bias[h] = full[2 * ch : 2 * ch + 8]
    for copy in lat_out:
        copy.wait_recv()
    q_gain = qg[...] * (HD ** (-0.5) * math.log2(math.e))
    k_gain = kg[...]
    block_rows = 4 * half

    def image_block(side, carry):
        block = jnp.concatenate([lall[side, k] for k in range(4)], axis=0)
        block = jnp.concatenate([block, block], axis=1)
        at = pl.ds(pl.multiple_of(side * block_rows, block_rows), block_rows)
        for h in range(heads):
            x = dot(block, rhs[h]) + (bias[h, 0:1, :] + bias[h, 1:2, :])
            q[h, at, :] = head_norm(x[:, 0:HD], q_gain).astype(BF16)
            kv[h, at, 0:HD] = head_norm(x[:, HD : 2 * HD], k_gain).astype(BF16)
            kv[h, at, HD : 2 * HD] = x[:, 2 * HD :].astype(BF16) * mask[at, :]
        return carry

    lax.fori_loop(0, 2, image_block, 0)
    kv_img = [
        remote(
            kv.at[h, pl.ds(0, img)], kvm.at[h, pl.ds(0, img)], ks.at[h], kr.at[h],
            {"group": mate},
        )
        for h in range(heads)
    ]
    for copy in kv_img:
        copy.start()

    def text_block(first, count):
        span = slice(img + first * trows, img + (first + count) * trows)
        lhs_t = txt[first] if count == 1 else jnp.concatenate(
            [txt[first + k] for k in range(count)], axis=0
        )
        copies = []
        for h in range(heads):
            x = dot(lhs_t, wt[:, h * 2 * HD : (h + 1) * 2 * HD])
            kv[h, span, 0:HD] = head_norm(x[:, 0:HD], k_gain).astype(BF16)
            kv[h, span, HD : 2 * HD] = x[:, HD:].astype(BF16) * mask[span, :]
            i = heads + (first if first < 2 else 2) * heads + h
            rows_t = pl.ds(img + first * trows, count * trows)
            copy = remote(
                kv.at[h, rows_t], kvm.at[h, rows_t], ks.at[i], kr.at[i], {"group": mate}
            )
            copy.start()
            copies.append(copy)
        return copies

    c_wt.wait()
    kv_txt = text_block(0, 1)
    on = flag.astype(BF16)

    def keys(h, parts):
        return jnp.concatenate([ref[h, lo : lo + n, 0:HD] for ref, lo, n in parts], axis=0)

    def values(h, parts):
        rows_v = []
        for ref, lo, n in parts:
            v = ref[h, lo : lo + n, HD : 2 * HD]
            if ref is kvm:
                v = v * on
            live = (maskm if ref is kvm else mask)[lo : lo + n, :]
            rows_v.append(jnp.concatenate([v, live], axis=1))
        return jnp.concatenate(rows_v, axis=0)

    def attend(h, at, parts):
        p = jnp.exp2(nt_dot(q[h, at, :], keys(h, parts))).astype(BF16)
        return dot(p, values(h, parts))

    def each_side(fn):
        def run(side, carry):
            at = pl.ds(pl.multiple_of(side * block_rows, block_rows), block_rows)
            for h in range(heads):
                fn(h, at)
            return carry

        lax.fori_loop(0, 2, run, 0)

    def own_image(h, at):
        acc[h, at, :] = attend(h, at, [(kv, 0, img)])

    each_side(own_image)

    to_right[0].wait_recv()
    norm_text(0, slot=2)
    on_right[0].start()
    to_left[2].wait_recv()
    norm_text(2, slot=1)
    on_left[0].start()
    for copy in kv_img:
        copy.wait_recv()

    def mate_image(h, at):
        acc[h, at, :] += attend(h, at, [(kvm, 0, img)])

    each_side(mate_image)

    to_right[1].wait_recv()
    on_right[1].start()
    to_left[3].wait_recv()
    on_left[1].start()
    to_right[2].wait_recv()
    to_right[3].wait_recv()
    to_left[0].wait_recv()
    to_left[1].wait_recv()
    kv_txt += text_block(1, 2)
    for copy in kv_txt:
        copy.wait_recv()

    def most_text(h, at):
        acc[h, at, :] += attend(h, at, [(kv, img, 3 * trows), (kvm, img, 3 * trows)])

    each_side(most_text)

    for copy in on_right + on_left:
        copy.wait_recv()
    kv_last = text_block(3, 1)
    last = img + 3 * trows

    mixes = []
    for side in range(2):
        copies = {k: [] for k in (1, 2, 3)}
        for h in range(heads):
            if side == 0:
                kv_last[h].wait_recv()
            at = slice(side * block_rows, (side + 1) * block_rows)
            total = acc[h, at, :] + attend(h, at, [(kv, last, trows), (kvm, last, trows)])
            share = (total[:, 0:HD] / total[:, HD : 2 * HD]).astype(BF16)
            for k in range(4):
                mix[side, k, h] = share[k * half : (k + 1) * half]
            for k in (2, 1, 3):
                i = (side * 3 + k - 1) * heads + h
                copy = remote(
                    mix.at[side, k, h], mixr.at[side, 3 - k, h], ms.at[i], mr.at[i],
                    {"mp": lax.rem(m + k, n_mp)},
                )
                copy.start()
                copies[k].append(copy)
        mixes.append(copies)

    def project(side, ref, k, first):
        base = pl.multiple_of(lax.rem(m + k, n_mp) * (heads * HD), heads * HD)
        own = jnp.concatenate([ref[h] for h in range(heads)], axis=1)
        for j in range(d // wide):
            cols = slice(j * wide, (j + 1) * wide)
            x = dot(own, wo[pl.ds(base, heads * HD), cols])
            att[side, :, cols] = x if first else att[side, :, cols] + x

    def finish(side):
        small = min(half, 32)
        for i in range(half // small):
            at = slice(i * small, (i + 1) * small)
            x = xc[side, at, :] + mimg[2, pl.ds(step, 1), :] * att[side, at, :]
            center = x - jnp.mean(x, -1, keepdims=True)
            spread = jnp.mean(center * center, -1, keepdims=True)
            y = center * lax.rsqrt(spread + 1e-06) * (1.0 + mfin[step, 1:2, :]) + mfin[step, 0:1, :]
            fin[at, :] = y.astype(BF16)
        return nt_dot(wf[...], fin[...])

    c_wo.wait()
    project(0, mix.at[0, 0], 0, True)
    project(1, mix.at[1, 0], 0, True)
    c_wf.wait()
    c_mfin.wait()
    for k in (2, 1, 3):
        for copy in mixes[0][k]:
            copy.wait_recv()
        project(0, mixr.at[0, 3 - k], 4 - k, False)
    vsend[...] = finish(0)
    swap = remote(vsend, vrecv, vs.at[0], vr.at[0], {"cfg": 1 - c})
    swap.start()
    for k in (2, 1, 3):
        for copy in mixes[1][k]:
            copy.wait_recv()
        project(1, mixr.at[1, 3 - k], 4 - k, False)
    own = finish(1)
    swap.wait_recv()
    other = vrecv[...]
    cond = jnp.where(c == 0, own, other)
    uncond = jnp.where(c == 0, other, own)
    guided = uncond + guide[g] * (cond - uncond)
    spot = lax.broadcasted_iota(jnp.int32, (ch, half), 1) + (m * rows + c * half)
    guided = jnp.where(spot < il, guided, 0.0)
    out[0] = guided
    out[1] = lat[:, pl.ds(pl.multiple_of(c * half, half), half)] - step_size[step] * guided

    for copy in to_right + to_left + on_right + on_left + lat_out + kv_img + kv_txt + kv_last:
        copy.wait_send()
    for copies in mixes:
        for k in (2, 1, 3):
            for copy in copies[k]:
                copy.wait_send()
    swap.wait_send()


def unpack(both, velocity, moved):
    velocity[...] = both[0]
    moved[...] = both[1]


def local(
    latents, text_hidden, w_img_in, w_img_qkv, w_txt_kv, q_gain, k_gain, w_out, w_final,
    mod_img, mod_txt, mod_final, guide, step_size, img_len, txt_len, split_flag, tstep,
):
    text = text_hidden[0]
    rows, ch = latents.shape
    trows, d = text.shape
    heads = w_img_qkv.shape[1] // (3 * HD)
    img, ntxt = 4 * rows, 4 * trows
    half = rows // 2
    hbm = pl.BlockSpec(memory_space=pl.ANY)
    vmem = pl.BlockSpec(memory_space=pltpu.VMEM)
    smem = pl.BlockSpec(memory_space=pltpu.SMEM)
    dma = pltpu.SemaphoreType.DMA
    out = jax.ShapeDtypeStruct((2, ch, half), F32)
    single = jax.ShapeDtypeStruct((ch, half), F32)
    scratch = [
        pltpu.VMEM((ch, rows), F32),
        pltpu.VMEM(text.shape, BF16),
        pltpu.VMEM(w_img_in.shape, BF16),
        pltpu.VMEM((heads, d, 3 * HD), BF16),
        pltpu.VMEM(w_txt_kv.shape, BF16),
        pltpu.VMEM(w_out.shape, BF16),
        pltpu.VMEM((ch, d), BF16),
        pltpu.VMEM((3, mod_img.shape[0], d), F32),
        pltpu.VMEM(mod_txt.shape, F32),
        pltpu.VMEM(mod_final.shape, F32),
        pltpu.VMEM((4, trows, d), BF16),
        pltpu.VMEM((2, 4, half, 2 * ch), BF16),
        pltpu.VMEM((2 * ch, d), BF16),
        pltpu.VMEM((2 * ch + 16, d), BF16),
        pltpu.VMEM((heads, 4 * ch, 3 * HD), BF16),
        pltpu.VMEM((heads, 8, 3 * HD), F32),
        pltpu.VMEM((2, half, d), F32),
        pltpu.VMEM((heads, img, HD), BF16),
        pltpu.VMEM((heads, img + ntxt, 2 * HD), BF16),
        pltpu.VMEM((heads, img + ntxt, 2 * HD), BF16),
        pltpu.VMEM((img + ntxt, HD), BF16),
        pltpu.VMEM((img + ntxt, HD), BF16),
        pltpu.VMEM((heads, img, 2 * HD), F32),
        pltpu.VMEM((2, half, d), F32),
        pltpu.VMEM((2, 4, heads, half, HD), BF16),
        pltpu.VMEM((2, 3, heads, half, HD), BF16),
        pltpu.VMEM((half, d), BF16),
        pltpu.VMEM((ch, half), F32),
        pltpu.VMEM((ch, half), F32),
        dma((13 + heads,)),
        dma((12,)), dma((12,)),
        dma((3,)), dma((3,)),
        dma((4 * heads,)), dma((4 * heads,)),
        dma((6 * heads,)), dma((6 * heads,)),
        dma((1,)), dma((1,)),
    ]
    both = pl.pallas_call(
        body,
        out_shape=out,
        in_specs=[hbm] * 10 + [vmem] * 2 + [smem] * 6,
        out_specs=vmem,
        scratch_shapes=scratch,
        compiler_params=pltpu.CompilerParams(
            collective_id=0, has_side_effects=True, vmem_limit_bytes=61 * 1024 * 1024
        ),
        name="guided_step",
    )(
        latents.T, text, w_img_in, w_img_qkv, w_txt_kv, w_out, w_final.T,
        jnp.transpose(mod_img, (1, 0, 2)), mod_txt, mod_final,
        q_gain[None], k_gain[None], guide, step_size, img_len, txt_len, split_flag, tstep,
    )
    velocity, moved = pl.pallas_call(
        unpack,
        out_shape=(single, single),
        in_specs=[vmem],
        out_specs=(vmem, vmem),
        name="unpack",
    )(both)
    return velocity.T[None], moved.T[None]


def solution(mesh):
    rep = P()
    placed = (
        P(("group", "mp"), None), P("cfg", ("group", "mp"), None), rep,
        P(None, "mp"), P(None, "mp"),
    ) + (rep,) * 13
    out = P("cfg", ("group", "mp"), None)
    return jax.shard_map(
        local, mesh=mesh, in_specs=placed, out_specs=(out, out), check_vma=False
    )
```

```python
import functools
import math

import jax
import jax.numpy as jnp
from jax import lax
from jax.experimental import pallas as pl
from jax.experimental.pallas import tpu as pltpu
from jax.sharding import PartitionSpec as P

HD = 128
F32 = jnp.float32
BF16 = jnp.bfloat16
MESH = pl.DeviceIdType.MESH
TEXT_FROM = (0, 1, 3, 2)


def nt_dot(a, b):
    return lax.dot_general(a, b, (((1,), (1,)), ((), ())), preferred_element_type=F32)


def dot(a, b):
    return jnp.dot(a, b, preferred_element_type=F32)


def head_norm(values, gain):
    return values * lax.rsqrt(jnp.mean(values * values, -1, keepdims=True) + 1e-06) * gain


def split(values):
    high = values.astype(BF16)
    return high, (values - high.astype(F32)).astype(BF16)


def body(
    lat_h, text_h, win_h, wq_h, wt_h, wo_h, wf_h, mimg_h, mtxt_h, mfin_h,
    qg, kg, guide, step_size, img_len, txt_len, flags, tstep,
    out,
    lat, text, win, wq, wt, wo, wf, mimg, mtxt, mfin,
    txt, lall, wx, lhs, rhs, bias, xc, q, kv, kvm, mask, maskm, acc, att,
    mix, mixr, fin, vsend, vrecv,
    lsem, ts, tr, ls, lr, ks, kr, ms, mr, vs, vr,
):
    c = lax.axis_index("cfg")
    g = lax.axis_index("group")
    m = lax.axis_index("mp")
    n_mp = 4
    right, left = lax.rem(m + 1, n_mp), lax.rem(m + 3, n_mp)
    mate = g + 1 - 2 * lax.rem(g, 2)
    ch, rows = lat_h.shape
    trows, d = text_h.shape
    heads = wq_h.shape[1] // (3 * HD)
    img, ntxt = rows * n_mp, trows * n_mp
    half = rows // 2
    part = trows // 4

    def chunk(i):
        return pl.ds(i * part, part)

    def local_copy(src, dst, i):
        copy = pltpu.make_async_copy(src, dst, lsem.at[i])
        copy.start()
        return copy

    c_lat = local_copy(lat_h, lat, 2)
    c_win = local_copy(win_h, win, 3)
    c_mtxt = local_copy(mtxt_h, mtxt, 1)
    c_text = local_copy(text_h, text, 0)
    c_mimg = local_copy(mimg_h, mimg, 4)

    barrier = pltpu.get_barrier_semaphore()
    for k in (1, 2, 3):
        pl.semaphore_signal(
            barrier, inc=1, device_id={"mp": lax.rem(m + k, n_mp)}, device_id_type=MESH
        )
    pl.semaphore_signal(barrier, inc=1, device_id={"group": mate}, device_id_type=MESH)
    pl.semaphore_signal(barrier, inc=1, device_id={"cfg": 1 - c}, device_id_type=MESH)

    def remote(src, dst, ssem, rsem, device):
        return pltpu.make_async_remote_copy(
            src_ref=src, dst_ref=dst, send_sem=ssem, recv_sem=rsem,
            device_id=device, device_id_type=MESH,
        )

    step = tstep[g]
    il, tl = img_len[g], txt_len[g]
    il_m, tl_m = img_len[mate], txt_len[mate]
    flag = jnp.where(flags[c, g] == 1, 1.0, 0.0).astype(F32)

    def source(i, first):
        return text_h.at[chunk(i)] if i == first else txt.at[0, chunk(i)]

    to_right = [
        remote(source(i, 0), txt.at[2, chunk(i)], ts.at[i], tr.at[i], {"mp": right})
        for i in range(4)
    ]
    to_left = [
        remote(source(i, 2), txt.at[1, chunk(i)], ts.at[4 + i], tr.at[4 + i], {"mp": left})
        for i in range(4)
    ]
    on_right = [
        remote(txt.at[2, chunk(i)], txt.at[3, chunk(i)], ts.at[8 + i], tr.at[8 + i], {"mp": right})
        for i in (0, 1)
    ]
    on_left = [
        remote(txt.at[1, chunk(i)], txt.at[3, chunk(i)], ts.at[8 + i], tr.at[8 + i], {"mp": left})
        for i in (2, 3)
    ]

    def norm_text(i, slot=0):
        x = (text[chunk(i), :] if slot == 0 else txt[slot, chunk(i), :]).astype(F32)
        center = x - jnp.mean(x, -1, keepdims=True)
        spread = jnp.mean(center * center, -1, keepdims=True)
        y = center * lax.rsqrt(spread + 1e-06) * (1.0 + mtxt[step, 1:2, :]) + mtxt[step, 0:1, :]
        txt[slot, chunk(i), :] = y.astype(BF16)

    pl.semaphore_wait(barrier, 5)
    to_right[0].start()
    to_left[2].start()
    c_lat.wait()
    c_win.wait()

    e_row = lax.broadcasted_iota(jnp.int32, (ch, 2 * ch), 0)
    e_col = lax.broadcasted_iota(jnp.int32, (ch, 2 * ch), 1)
    twice = jnp.where((e_col == e_row) | (e_col == e_row + ch), 1.0, 0.0).astype(BF16)
    lat2 = lax.dot_general(
        lat[...].astype(BF16), twice, (((0,), (0,)), ((), ())), preferred_element_type=F32
    )
    w = win[...].astype(F32)
    w = w - jnp.mean(w, -1, keepdims=True)
    w_high, w_low = split(w)
    wx[0:ch, :] = w_high
    wx[ch : 2 * ch, :] = w_low
    lat2b = lat2.astype(BF16)
    squares = jnp.zeros((rows, HD), F32)
    wide = min(d, 512)
    for j in range(d // wide):
        x = dot(lat2b, wx[:, j * wide : (j + 1) * wide])
        xc[1 - c, :, j * wide : (j + 1) * wide] = x[0:half]
        xc[c, :, j * wide : (j + 1) * wide] = x[half:]
        for k in range(wide // HD):
            piece = x[:, k * HD : (k + 1) * HD]
            squares = squares + piece * piece
    rstd = lax.rsqrt(jnp.sum(squares, -1, keepdims=True) / d + 1e-06)
    scaled = lat2 * rstd
    scaled_high = scaled.astype(BF16).astype(F32)
    lane = lax.broadcasted_iota(jnp.int32, (rows, 2 * ch), 1)
    scaled = jnp.where(lane < ch, scaled_high, scaled - scaled_high).astype(BF16)
    lall[1 - c, 0] = scaled[0:half]
    lall[c, 0] = scaled[half:]
    lat_out = [
        remote(
            lall.at[:, 0], lall.at[:, 4 - k], ls.at[k - 1], lr.at[k - 1],
            {"mp": lax.rem(m + k, n_mp)},
        )
        for k in (1, 2, 3)
    ]
    for copy in lat_out:
        copy.start()

    c_mtxt.wait()
    c_text.wait()
    c_mimg.wait()
    c_wq = [
        local_copy(wq_h.at[:, pl.ds(h * 3 * HD, 3 * HD)], wq.at[h], 5 + h) for h in range(heads)
    ]
    c_wt = local_copy(wt_h, wt, 5 + heads)
    norm_text(1)
    to_right[1].start()
    norm_text(3)
    to_left[3].start()
    norm_text(2)
    to_right[2].start()
    norm_text(0)
    to_left[0].start()
    to_right[3].start()
    to_left[1].start()
    c_wo = local_copy(wo_h, wo, 6 + heads)
    c_wf = local_copy(wf_h, wf, 7 + heads)
    c_mfin = local_copy(mfin_h, mfin, 8 + heads)

    s_high, s_low = split(w * (1.0 + mimg[1, pl.ds(step, 1), :]))
    lhs[0:ch, :] = s_high
    lhs[ch : 2 * ch, :] = s_low
    b_high, b_low = split(mimg[0, pl.ds(step, 1), :])
    b_row = lax.broadcasted_iota(jnp.int32, (16, d), 0)
    lhs[2 * ch :, :] = jnp.where(
        b_row == 0, b_high.astype(F32), jnp.where(b_row == 1, b_low.astype(F32), 0.0)
    ).astype(BF16)

    def fill_mask(ref, img_live, txt_live, on):
        spot = lax.broadcasted_iota(jnp.int32, (half, HD), 0)
        for side in range(2):
            place = (1 - c) if side == 0 else c
            for k in range(4):
                start = lax.rem(m + k, n_mp) * rows + place * half
                at = side * 4 * half + k * half
                ref[at : at + half, :] = jnp.where(spot + start < img_live, on, 0.0).astype(BF16)
        spot_t = lax.broadcasted_iota(jnp.int32, (trows, HD), 0)
        for k in range(4):
            start = lax.rem(m + TEXT_FROM[k], n_mp) * trows
            ref[img + k * trows : img + (k + 1) * trows, :] = jnp.where(
                spot_t + start < txt_live, on, 0.0
            ).astype(BF16)

    fill_mask(mask, il, tl, 1.0)
    fill_mask(maskm, il_m, tl_m, flag)

    for h in range(heads):
        c_wq[h].wait()
        full = dot(lhs[...], wq[h])
        fold = full[0:ch] + full[ch : 2 * ch]
        high, low = split(fold)
        rhs[h, 0:ch, :] = high
        rhs[h, ch : 2 * ch, :] = high
        rhs[h, 2 * ch : 3 * ch, :] = low
        rhs[h, 3 * ch : 4 * ch, :] = low
        bias[h] = full[2 * ch : 2 * ch + 8]
    for copy in lat_out:
        copy.wait_recv()
    q_gain = qg[...] * (HD ** (-0.5) * math.log2(math.e))
    k_gain = kg[...]
    block_rows = 4 * half

    def image_block(side, carry):
        block = jnp.concatenate([lall[side, k] for k in range(4)], axis=0)
        block = jnp.concatenate([block, block], axis=1)
        at = pl.ds(pl.multiple_of(side * block_rows, block_rows), block_rows)
        for h in range(heads):
            x = dot(block, rhs[h]) + (bias[h, 0:1, :] + bias[h, 1:2, :])
            q[h, at, :] = head_norm(x[:, 0:HD], q_gain).astype(BF16)
            kv[h, at, 0:HD] = head_norm(x[:, HD : 2 * HD], k_gain).astype(BF16)
            kv[h, at, HD : 2 * HD] = x[:, 2 * HD :].astype(BF16) * mask[at, :]
        return carry

    lax.fori_loop(0, 2, image_block, 0)
    kv_img = [
        remote(
            kv.at[h, pl.ds(0, img)], kvm.at[h, pl.ds(0, img)], ks.at[h], kr.at[h],
            {"group": mate},
        )
        for h in range(heads)
    ]
    for copy in kv_img:
        copy.start()

    def text_block(first, count):
        span = slice(img + first * trows, img + (first + count) * trows)
        lhs_t = txt[first] if count == 1 else jnp.concatenate(
            [txt[first + k] for k in range(count)], axis=0
        )
        copies = []
        for h in range(heads):
            x = dot(lhs_t, wt[:, h * 2 * HD : (h + 1) * 2 * HD])
            kv[h, span, 0:HD] = head_norm(x[:, 0:HD], k_gain).astype(BF16)
            kv[h, span, HD : 2 * HD] = x[:, HD:].astype(BF16) * mask[span, :]
            i = heads + (first if first < 2 else 2) * heads + h
            rows_t = pl.ds(img + first * trows, count * trows)
            copy = remote(
                kv.at[h, rows_t], kvm.at[h, rows_t], ks.at[i], kr.at[i], {"group": mate}
            )
            copy.start()
            copies.append(copy)
        return copies

    c_wt.wait()
    kv_txt = text_block(0, 1)
    to_right[0].wait_recv()
    norm_text(0, slot=2)
    on_right[0].start()
    to_left[2].wait_recv()
    norm_text(2, slot=1)
    on_left[0].start()
    on = flag.astype(BF16)

    def keys(h, parts):
        return jnp.concatenate([ref[h, lo : lo + n, 0:HD] for ref, lo, n in parts], axis=0)

    def values(h, parts):
        rows_v = []
        for ref, lo, n in parts:
            v = ref[h, lo : lo + n, HD : 2 * HD]
            if ref is kvm:
                v = v * on
            live = (maskm if ref is kvm else mask)[lo : lo + n, :]
            rows_v.append(jnp.concatenate([v, live], axis=1))
        return jnp.concatenate(rows_v, axis=0)

    def attend(h, at, parts):
        p = jnp.exp2(nt_dot(q[h, at, :], keys(h, parts))).astype(BF16)
        return dot(p, values(h, parts))

    def each_side(fn):
        def run(side, carry):
            at = pl.ds(pl.multiple_of(side * block_rows, block_rows), block_rows)
            for h in range(heads):
                fn(h, at)
            return carry

        lax.fori_loop(0, 2, run, 0)

    def own_image(h, at):
        acc[h, at, :] = attend(h, at, [(kv, 0, img)])

    each_side(own_image)

    for copy in kv_img:
        copy.wait_recv()

    def mate_image(h, at):
        acc[h, at, :] += attend(h, at, [(kvm, 0, img)])

    each_side(mate_image)

    to_right[1].wait_recv()
    on_right[1].start()
    to_left[3].wait_recv()
    on_left[1].start()
    to_right[2].wait_recv()
    to_right[3].wait_recv()
    to_left[0].wait_recv()
    to_left[1].wait_recv()
    kv_txt += text_block(1, 2)
    for copy in kv_txt:
        copy.wait_recv()

    def most_text(h, at):
        acc[h, at, :] += attend(h, at, [(kv, img, 3 * trows), (kvm, img, 3 * trows)])

    each_side(most_text)

    for copy in on_right + on_left:
        copy.wait_recv()
    kv_last = text_block(3, 1)
    last = img + 3 * trows

    mixes = []
    for side in range(2):
        copies = {k: [] for k in (1, 2, 3)}
        for h in range(heads):
            if side == 0:
                kv_last[h].wait_recv()
            at = slice(side * block_rows, (side + 1) * block_rows)
            total = acc[h, at, :] + attend(h, at, [(kv, last, trows), (kvm, last, trows)])
            share = (total[:, 0:HD] / total[:, HD : 2 * HD]).astype(BF16)
            for k in range(4):
                mix[side, k, h] = share[k * half : (k + 1) * half]
            for k in (2, 1, 3):
                i = (side * 3 + k - 1) * heads + h
                copy = remote(
                    mix.at[side, k, h], mixr.at[side, 3 - k, h], ms.at[i], mr.at[i],
                    {"mp": lax.rem(m + k, n_mp)},
                )
                copy.start()
                copies[k].append(copy)
        mixes.append(copies)

    def project(side, ref, k, first):
        base = pl.multiple_of(lax.rem(m + k, n_mp) * (heads * HD), heads * HD)
        own = jnp.concatenate([ref[h] for h in range(heads)], axis=1)
        for j in range(d // wide):
            cols = slice(j * wide, (j + 1) * wide)
            x = dot(own, wo[pl.ds(base, heads * HD), cols])
            att[side, :, cols] = x if first else att[side, :, cols] + x

    def finish(side):
        small = min(half, 32)
        for i in range(half // small):
            at = slice(i * small, (i + 1) * small)
            x = xc[side, at, :] + mimg[2, pl.ds(step, 1), :] * att[side, at, :]
            center = x - jnp.mean(x, -1, keepdims=True)
            spread = jnp.mean(center * center, -1, keepdims=True)
            y = center * lax.rsqrt(spread + 1e-06) * (1.0 + mfin[step, 1:2, :]) + mfin[step, 0:1, :]
            fin[at, :] = y.astype(BF16)
        return nt_dot(wf[...], fin[...])

    c_wo.wait()
    project(0, mix.at[0, 0], 0, True)
    project(1, mix.at[1, 0], 0, True)
    c_wf.wait()
    c_mfin.wait()
    for k in (2, 1, 3):
        for copy in mixes[0][k]:
            copy.wait_recv()
        project(0, mixr.at[0, 3 - k], 4 - k, False)
    vsend[...] = finish(0)
    swap = remote(vsend, vrecv, vs.at[0], vr.at[0], {"cfg": 1 - c})
    swap.start()
    for k in (2, 1, 3):
        for copy in mixes[1][k]:
            copy.wait_recv()
        project(1, mixr.at[1, 3 - k], 4 - k, False)
    own = finish(1)
    swap.wait_recv()
    other = vrecv[...]
    cond = jnp.where(c == 0, own, other)
    uncond = jnp.where(c == 0, other, own)
    guided = uncond + guide[g] * (cond - uncond)
    spot = lax.broadcasted_iota(jnp.int32, (ch, half), 1) + (m * rows + c * half)
    guided = jnp.where(spot < il, guided, 0.0)
    out[0] = guided
    out[1] = lat[:, pl.ds(pl.multiple_of(c * half, half), half)] - step_size[step] * guided

    for copy in to_right + to_left + on_right + on_left + lat_out + kv_img + kv_txt + kv_last:
        copy.wait_send()
    for copies in mixes:
        for k in (2, 1, 3):
            for copy in copies[k]:
                copy.wait_send()
    swap.wait_send()


def unpack(both, velocity, moved):
    velocity[...] = both[0]
    moved[...] = both[1]


def local(
    latents, text_hidden, w_img_in, w_img_qkv, w_txt_kv, q_gain, k_gain, w_out, w_final,
    mod_img, mod_txt, mod_final, guide, step_size, img_len, txt_len, split_flag, tstep,
):
    text = text_hidden[0]
    rows, ch = latents.shape
    trows, d = text.shape
    heads = w_img_qkv.shape[1] // (3 * HD)
    img, ntxt = 4 * rows, 4 * trows
    half = rows // 2
    hbm = pl.BlockSpec(memory_space=pl.ANY)
    vmem = pl.BlockSpec(memory_space=pltpu.VMEM)
    smem = pl.BlockSpec(memory_space=pltpu.SMEM)
    dma = pltpu.SemaphoreType.DMA
    out = jax.ShapeDtypeStruct((2, ch, half), F32)
    single = jax.ShapeDtypeStruct((ch, half), F32)
    scratch = [
        pltpu.VMEM((ch, rows), F32),
        pltpu.VMEM(text.shape, BF16),
        pltpu.VMEM(w_img_in.shape, BF16),
        pltpu.VMEM((heads, d, 3 * HD), BF16),
        pltpu.VMEM(w_txt_kv.shape, BF16),
        pltpu.VMEM(w_out.shape, BF16),
        pltpu.VMEM((ch, d), BF16),
        pltpu.VMEM((3, mod_img.shape[0], d), F32),
        pltpu.VMEM(mod_txt.shape, F32),
        pltpu.VMEM(mod_final.shape, F32),
        pltpu.VMEM((4, trows, d), BF16),
        pltpu.VMEM((2, 4, half, 2 * ch), BF16),
        pltpu.VMEM((2 * ch, d), BF16),
        pltpu.VMEM((2 * ch + 16, d), BF16),
        pltpu.VMEM((heads, 4 * ch, 3 * HD), BF16),
        pltpu.VMEM((heads, 8, 3 * HD), F32),
        pltpu.VMEM((2, half, d), F32),
        pltpu.VMEM((heads, img, HD), BF16),
        pltpu.VMEM((heads, img + ntxt, 2 * HD), BF16),
        pltpu.VMEM((heads, img + ntxt, 2 * HD), BF16),
        pltpu.VMEM((img + ntxt, HD), BF16),
        pltpu.VMEM((img + ntxt, HD), BF16),
        pltpu.VMEM((heads, img, 2 * HD), F32),
        pltpu.VMEM((2, half, d), F32),
        pltpu.VMEM((2, 4, heads, half, HD), BF16),
        pltpu.VMEM((2, 3, heads, half, HD), BF16),
        pltpu.VMEM((half, d), BF16),
        pltpu.VMEM((ch, half), F32),
        pltpu.VMEM((ch, half), F32),
        dma((13 + heads,)),
        dma((12,)), dma((12,)),
        dma((3,)), dma((3,)),
        dma((4 * heads,)), dma((4 * heads,)),
        dma((6 * heads,)), dma((6 * heads,)),
        dma((1,)), dma((1,)),
    ]
    both = pl.pallas_call(
        body,
        out_shape=out,
        in_specs=[hbm] * 10 + [vmem] * 2 + [smem] * 6,
        out_specs=vmem,
        scratch_shapes=scratch,
        compiler_params=pltpu.CompilerParams(
            collective_id=0, has_side_effects=True, vmem_limit_bytes=61 * 1024 * 1024
        ),
        name="guided_step",
    )(
        latents.T, text, w_img_in, w_img_qkv, w_txt_kv, w_out, w_final.T,
        jnp.transpose(mod_img, (1, 0, 2)), mod_txt, mod_final,
        q_gain[None], k_gain[None], guide, step_size, img_len, txt_len, split_flag, tstep,
    )
    velocity, moved = pl.pallas_call(
        unpack,
        out_shape=(single, single),
        in_specs=[vmem],
        out_specs=(vmem, vmem),
        name="unpack",
    )(both)
    return velocity.T[None], moved.T[None]


def solution(mesh):
    rep = P()
    placed = (
        P(("group", "mp"), None), P("cfg", ("group", "mp"), None), rep,
        P(None, "mp"), P(None, "mp"),
    ) + (rep,) * 13
    out = P("cfg", ("group", "mp"), None)
    return jax.shard_map(
        local, mesh=mesh, in_specs=placed, out_specs=(out, out), check_vma=False
    )
```
